256 devices in a mesh: grp: 64 (over z, y, core), head: 4 (over x).
Axes of the slice: x: 4, y: 4, z: 8, core: 2. Of those that a mesh axis runs over, the one named last changes fastest.
Arguments:
- arriving_hiddens: bfloat16 [512, 4, 2048], P('grp', None, 'head'), may hold values from -6 to 6
- occupied_slot_totals: int32 [512], P('grp'), may hold values from 1 to 4
- former_indices: int32 [512], P('grp'), may hold values from 0 to 511, as said below
- reconstruct_marks: int32 [512], P('grp'), may hold values from 0 to 1, as said below
- retained_hiddens: bfloat16 [512, 32, 2048], P('grp', None, 'head'), may hold values from -6 to 6
- carried_memory_matrices: float32 [512, 16, 64, 64], P('grp', 'head'), may hold values from -12 to 12
- lagged_previous_entries: float32 [512, 2, 2048], P('grp', None, 'head'), may hold values from -6 to 6
- pre_attention_scaling: float32 [2048], replicated, may hold values from 0.5 to 1.5
- pre_feedforward_scaling: float32 [2048], replicated, may hold values from 0.5 to 1.5
- lag_blend_fractions: float32 [5, 2048], replicated, may hold values from 0 to 1
- acceptance_projection: bfloat16 [2048, 1024], P(None, 'head'), may hold values from -0.125 to 0.125
- address_projection: bfloat16 [2048, 1024], P(None, 'head'), may hold values from -0.125 to 0.125
- content_projection: bfloat16 [2048, 1024], P(None, 'head'), may hold values from -0.125 to 0.125
- fading_lowrank_left: bfloat16 [2048, 64], replicated, may hold values from -0.125 to 0.125
- fading_lowrank_right: bfloat16 [64, 1024], P(None, 'head'), may hold values from -0.75 to 0.75
- fading_baseline_entries: float32 [1024], P('head'), may hold values from -6 to 1
- present_item_reward: float32 [1024], P('head'), may hold values from -6 to 6
- grouped_layer_scaling: float32 [1024], P('head'), may hold values from 0.5 to 1.5
- attention_exit_projection: bfloat16 [1024, 2048], P('head'), may hold values from -0.1875 to 0.1875
- feedforward_address_proj: bfloat16 [2048, 3584], P(None, 'head'), may hold values from -0.125 to 0.125
- feedforward_content_proj: bfloat16 [3584, 2048], P('head'), may hold values from -0.09375 to 0.09375
Outputs:
- next_tokens: bfloat16 [512, 4, 2048], P('grp', None, 'head')
- next_state: float32 [512, 16, 64, 64], P('grp', 'head')
- next_shift: float32 [512, 2, 2048], P('grp', None, 'head')
The draws below stay inside these ranges and needn't reach their ends.
Inputs may be any that keep to these rules, and one draw needn't show every extreme that they name: former_indices[g * 8 + j] = ((g + offset_j) mod 64) * 8 + local_j, where the 8 offsets offset_j are distinct numbers of 0 to 63 and local_j is a permutation of 0 to 7, both the same for every group g. `reconstruct_marks`: among the 8 requests of one group at most 2 are marked, and some group has exactly 2.
All inputs are finite; a program needn't handle non-finite values.
Results may differ from the reference program's by a relative error of at most 0.028.
Values may be sent and summed in bfloat16 or wider, within the bound.
No kernel may reach another device: no remote copies, remote signals or barrier semaphores. Data moves between devices by JAX's collectives and lax.ppermute only.
A program may use at most 128 MiB of HBM per device.

```python
import jax
import jax.numpy as jnp
from jax import lax

MODEL_DIM = 2048
ATTENTION_WIDTH = 64
DECAY_INNER = 64
RESIDENT_GROUPS = 16
FF = 3584
STEPS = 4
HIST = 32
R_GRP = 8
REB = 2
REQ = 512
N_GRP = 64


def draw_former_indices(key, part):
    key_first, key_second = jax.random.split(jax.random.fold_in(key, 17))
    offsets = jax.random.permutation(key_first, N_GRP)[:R_GRP].astype(jnp.int32)
    local_rows = jax.random.permutation(key_second, R_GRP).astype(jnp.int32)
    groups = jnp.arange(N_GRP, dtype=jnp.int32)[:, None]
    former_indices = (groups + offsets[None, :]) % N_GRP * R_GRP + local_rows[None, :]
    return former_indices.reshape(-1).astype(jnp.int32)


def group_order(key):
    return jax.random.permutation(key, R_GRP).astype(jnp.int32)


def draw_reconstruct_marks(key, part):
    key_first, key_second, key_third = jax.random.split(jax.random.fold_in(key, 29), 3)
    group_counts = jax.random.randint(key_first, (N_GRP,), 0, REB + 1)
    busiest = jax.random.randint(key_second, (), 0, N_GRP)
    group_counts = jnp.where(jnp.arange(N_GRP) == busiest, REB, group_counts)
    orders = jax.vmap(group_order)(jax.random.split(key_third, N_GRP))
    marks_table = (orders < group_counts[:, None]).astype(jnp.int32)
    return marks_table.reshape(-1)


def set_ends(values, rng, smallest, high):
    place = [jax.random.randint(jax.random.fold_in(rng, axis), (), 0, length) for axis, length in enumerate(values.shape)]
    main_axis = values.shape.index(max(values.shape))
    beside = place[:main_axis] + [(place[main_axis] + 1) % values.shape[main_axis]] + place[main_axis + 1:]
    return values.at[tuple(place)].set(smallest).at[tuple(beside)].set(high)


def block_levels(own_key, extent, pieces, low, largest):
    def one(dim, blocks):
        heights = jax.random.uniform(jax.random.fold_in(jax.random.fold_in(own_key, 6), dim), (blocks,), jnp.float32, low / len(pieces), largest / len(pieces))
        return jnp.repeat(jnp.exp(heights), extent[dim] // blocks).reshape((-1,) + (1,) * (len(extent) - dim - 1))

    level = one(*pieces[0])
    for cut in pieces[1:]:
        level = level * one(*cut)
    return level


def gaussian(rng, shape, scale, reach, cuts=(), kind=jnp.bfloat16):
    drawn = jax.random.normal(rng, shape, jnp.float32) * scale
    if len(cuts) > 0:
        drawn = block_levels(rng, shape, cuts, -0.22, 0.18) * drawn
    return jnp.clip(drawn, min=-reach, max=reach).astype(kind)


def setup_inputs(seed: int = 0) -> dict:
    streams_of = jax.random.split(jax.random.key(seed), 22)
    arriving_hiddens = gaussian(streams_of[0], (REQ, STEPS, MODEL_DIM), 1.0, 6.0, ((0, 64), (2, 4)))
    occupied_slot_totals = set_ends(jax.random.randint(streams_of[1], (REQ,), 1, 5), jax.random.fold_in(streams_of[1], 1), 1, 4).astype(jnp.int32)
    former_indices = draw_former_indices(jax.random.fold_in(streams_of[21], 71), 0)
    reconstruct_marks = draw_reconstruct_marks(jax.random.fold_in(streams_of[21], 71), 0)
    retained_hiddens = gaussian(streams_of[4], (REQ, HIST, MODEL_DIM), 1.0, 6.0, ((0, 64), (2, 4)))
    carried_memory_matrices = gaussian(streams_of[5], (REQ, RESIDENT_GROUPS, ATTENTION_WIDTH, ATTENTION_WIDTH), 2.0, 12.0, ((0, 64), (1, 4)), jnp.float32)
    lagged_previous_entries = gaussian(streams_of[6], (REQ, 2, MODEL_DIM), 1.0, 6.0, ((0, 64), (2, 4)), jnp.float32)
    pre_attention_scaling = jnp.clip(1.0 + 0.1 * jax.random.normal(streams_of[7], (MODEL_DIM,), jnp.float32), 0.5, 1.5)
    pre_feedforward_scaling = jnp.clip(1.0 + 0.1 * jax.random.normal(streams_of[8], (MODEL_DIM,), jnp.float32), 0.5, 1.5)
    lag_blend_fractions = jnp.clip(jax.random.uniform(streams_of[9], (5, MODEL_DIM), jnp.float32, 0.0, 1.0), 0.0, 1.0)
    acceptance_projection = gaussian(streams_of[10], (MODEL_DIM, RESIDENT_GROUPS * ATTENTION_WIDTH), MODEL_DIM ** -0.5, 0.125, ((1, 4),))
    address_projection = gaussian(streams_of[11], (MODEL_DIM, RESIDENT_GROUPS * ATTENTION_WIDTH), MODEL_DIM ** -0.5, 0.125, ((1, 4),))
    content_projection = gaussian(streams_of[12], (MODEL_DIM, RESIDENT_GROUPS * ATTENTION_WIDTH), MODEL_DIM ** -0.5, 0.125, ((1, 4),))
    fading_lowrank_left = gaussian(streams_of[13], (MODEL_DIM, DECAY_INNER), MODEL_DIM ** -0.5, 0.125)
    fading_lowrank_right = gaussian(streams_of[14], (DECAY_INNER, RESIDENT_GROUPS * ATTENTION_WIDTH), DECAY_INNER ** -0.5, 0.75, ((1, 4),))
    fading_baseline_entries = jnp.clip(-6.0 + 7.0 * jax.random.uniform(streams_of[15], (RESIDENT_GROUPS * ATTENTION_WIDTH,), jnp.float32) ** block_levels(streams_of[15], (RESIDENT_GROUPS * ATTENTION_WIDTH,), ((0, 4),), -0.2, 0.2), -6.0, 1.0)
    present_item_reward = gaussian(streams_of[16], (RESIDENT_GROUPS * ATTENTION_WIDTH,), 1.0, 6.0, ((0, 4),), jnp.float32)
    grouped_layer_scaling = jnp.clip(1.0 + 0.1 * jax.random.normal(streams_of[17], (RESIDENT_GROUPS * ATTENTION_WIDTH,), jnp.float32), 0.5, 1.5)
    attention_exit_projection = gaussian(streams_of[18], (RESIDENT_GROUPS * ATTENTION_WIDTH, MODEL_DIM), (RESIDENT_GROUPS * ATTENTION_WIDTH) ** -0.5, 0.1875, ((0, 4),))
    feedforward_address_proj = gaussian(streams_of[19], (MODEL_DIM, FF), MODEL_DIM ** -0.5, 0.125, ((1, 4),))
    feedforward_content_proj = gaussian(streams_of[20], (FF, MODEL_DIM), FF ** -0.5, 0.09375, ((0, 4),))
    return {"arriving_hiddens": arriving_hiddens, "occupied_slot_totals": occupied_slot_totals, "former_indices": former_indices, "reconstruct_marks": reconstruct_marks, "retained_hiddens": retained_hiddens, "carried_memory_matrices": carried_memory_matrices, "lagged_previous_entries": lagged_previous_entries, "pre_attention_scaling": pre_attention_scaling, "pre_feedforward_scaling": pre_feedforward_scaling, "lag_blend_fractions": lag_blend_fractions, "acceptance_projection": acceptance_projection, "address_projection": address_projection, "content_projection": content_projection, "fading_lowrank_left": fading_lowrank_left, "fading_lowrank_right": fading_lowrank_right, "fading_baseline_entries": fading_baseline_entries, "present_item_reward": present_item_reward, "grouped_layer_scaling": grouped_layer_scaling, "attention_exit_projection": attention_exit_projection, "feedforward_address_proj": feedforward_address_proj, "feedforward_content_proj": feedforward_content_proj}


EPSILON = 1e-05

def layer_norm(inputs, gain):
    centered = inputs - lax.optimization_barrier(jnp.mean(inputs, axis=-1, keepdims=True))
    spread = lax.optimization_barrier(jnp.mean(centered * centered, axis=-1, keepdims=True))
    return (centered * lax.rsqrt(spread + EPSILON) * gain).astype(jnp.bfloat16)

def blend_rows(current, previous, rate):
    return (current + (previous - current) * rate).astype(jnp.bfloat16)

def project(inputs, weight):
    flat_rows = inputs.reshape(-1, inputs.shape[-1])
    result = jnp.dot(flat_rows, weight, preferred_element_type=jnp.float32)
    return result.reshape(inputs.shape[:-1] + (weight.shape[1],))

def divide_into_groups(inputs):
    return inputs.reshape(inputs.shape[:-1] + (-1, ATTENTION_WIDTH))

def key_value_decay(current, previous, lag_blend_fractions, address_projection, content_projection, fading_lowrank_left, fading_lowrank_right, fading_baseline_entries):
    key_rows = project(blend_rows(current, previous, lag_blend_fractions[1]), address_projection)
    values = project(blend_rows(current, previous, lag_blend_fractions[2]), content_projection)
    lowrank = jnp.tanh(project(blend_rows(current, previous, lag_blend_fractions[3]), fading_lowrank_left)).astype(jnp.bfloat16)
    decay_rates = jnp.exp(-jnp.exp(fading_baseline_entries + project(lowrank, fading_lowrank_right)))
    return (divide_into_groups(key_rows), divide_into_groups(values), divide_into_groups(decay_rates))

def advance(present_outer_product, inputs):
    key_step, value_step, decay_step = inputs
    return (decay_step[..., :, None] * present_outer_product + key_step[..., :, None] * value_step[..., None, :], None)

def rebuild(retained_hiddens, pre_attention_scaling, lag_blend_fractions, address_projection, content_projection, fading_lowrank_left, fading_lowrank_right, fading_baseline_entries):
    standardized_entry = layer_norm(retained_hiddens.astype(jnp.float32), pre_attention_scaling)
    current = standardized_entry.astype(jnp.float32)
    previous = jnp.concatenate([jnp.zeros_like(current[:, :1]), current[:, :-1]], axis=1)
    key_rows, values, decay_rates = key_value_decay(current, previous, lag_blend_fractions, address_projection, content_projection, fading_lowrank_left, fading_lowrank_right, fading_baseline_entries)
    start_state = jnp.zeros(key_rows.shape[:1] + key_rows.shape[2:] + (ATTENTION_WIDTH,), jnp.float32)
    final_state, _ = lax.scan(advance, start_state, (jnp.moveaxis(key_rows, 1, 0), jnp.moveaxis(values, 1, 0), jnp.moveaxis(decay_rates, 1, 0)))
    return (final_state, current[:, -1])

def attention_result(standardized_entry, lagged_entry, present_outer_product, occupied_slot_totals, lag_blend_fractions, acceptance_projection, address_projection, content_projection, fading_lowrank_left, fading_lowrank_right, fading_baseline_entries, present_item_reward, grouped_layer_scaling):
    current = standardized_entry.astype(jnp.float32)
    previous = jnp.concatenate([lagged_entry[:, None], current[:, :-1]], axis=1)
    acceptance_gate_entries = divide_into_groups(project(blend_rows(current, previous, lag_blend_fractions[0]), acceptance_projection))
    key_rows, values, decay_rates = key_value_decay(current, previous, lag_blend_fractions, address_projection, content_projection, fading_lowrank_left, fading_lowrank_right, fading_baseline_entries)
    reward_grouped = divide_into_groups(present_item_reward)
    decoding_results = []
    for query_slot_index in range(current.shape[1]):
        address_content_product = key_rows[:, query_slot_index, :, :, None] * values[:, query_slot_index, :, None, :]
        decoding_results.append(jnp.einsum('ghl,ghlm->ghm', acceptance_gate_entries[:, query_slot_index], present_outer_product + reward_grouped[:, :, None] * address_content_product, precision=lax.Precision.HIGHEST))
        valid_rows = (query_slot_index < occupied_slot_totals)[:, None, None, None]
        present_outer_product = jnp.where(valid_rows, decay_rates[:, query_slot_index, :, :, None] * present_outer_product + address_content_product, present_outer_product)
    mixed_heads = jnp.stack(decoding_results, axis=1)
    centered = mixed_heads - lax.optimization_barrier(jnp.mean(mixed_heads, axis=-1, keepdims=True))
    spread = lax.optimization_barrier(jnp.mean(centered * centered, axis=-1, keepdims=True))
    grouped_results = (centered * lax.rsqrt(spread + EPSILON) * divide_into_groups(grouped_layer_scaling)).astype(jnp.bfloat16)
    return (grouped_results.reshape(grouped_results.shape[:2] + (-1,)), present_outer_product)

def last_live(inputs, occupied_slot_totals):
    pick_table = jnp.arange(inputs.shape[1])[None, :, None] == (occupied_slot_totals - 1)[:, None, None]
    return lax.optimization_barrier(jnp.sum(jnp.where(pick_table, inputs, jnp.zeros_like(inputs)), axis=1))

def reference(arriving_hiddens, occupied_slot_totals, former_indices, reconstruct_marks, retained_hiddens, carried_memory_matrices, lagged_previous_entries, pre_attention_scaling, pre_feedforward_scaling, lag_blend_fractions, acceptance_projection, address_projection, content_projection, fading_lowrank_left, fading_lowrank_right, fading_baseline_entries, present_item_reward, grouped_layer_scaling, attention_exit_projection, feedforward_address_proj, feedforward_content_proj):
    present_outer_product = jnp.take(carried_memory_matrices, former_indices, axis=0)
    shifts = jnp.take(lagged_previous_entries, former_indices, axis=0)
    rebuilt, last_hist = rebuild(retained_hiddens, pre_attention_scaling, lag_blend_fractions, address_projection, content_projection, fading_lowrank_left, fading_lowrank_right, fading_baseline_entries)
    marked = reconstruct_marks == 1
    present_outer_product = jnp.where(marked[:, None, None, None], rebuilt, present_outer_product)
    lagged_entry = jnp.where(marked[:, None], last_hist, shifts[:, 0])
    standardized_entry = layer_norm(arriving_hiddens.astype(jnp.float32), pre_attention_scaling)
    grouped_results, present_outer_product = attention_result(standardized_entry, lagged_entry, present_outer_product, occupied_slot_totals, lag_blend_fractions, acceptance_projection, address_projection, content_projection, fading_lowrank_left, fading_lowrank_right, fading_baseline_entries, present_item_reward, grouped_layer_scaling)
    middle = (arriving_hiddens.astype(jnp.float32) + project(grouped_results, attention_exit_projection)).astype(jnp.bfloat16)
    second = layer_norm(middle.astype(jnp.float32), pre_feedforward_scaling)
    current = second.astype(jnp.float32)
    previous = jnp.concatenate([shifts[:, 1][:, None], current[:, :-1]], axis=1)
    hidden = jnp.square(jax.nn.relu(project(blend_rows(current, previous, lag_blend_fractions[4]), feedforward_address_proj))).astype(jnp.bfloat16)
    result = (middle.astype(jnp.float32) + project(hidden, feedforward_content_proj)).astype(jnp.bfloat16)
    valid_rows = jnp.arange(arriving_hiddens.shape[1])[None, :] < occupied_slot_totals[:, None]
    result = jnp.where(valid_rows[..., None], result, jnp.zeros_like(result))
    next_shift = jnp.stack([last_live(standardized_entry.astype(jnp.float32), occupied_slot_totals), last_live(current, occupied_slot_totals)], axis=1)
    return (result, present_outer_product, next_shift)
```

```python
import functools

import jax
import jax.numpy as jnp
from jax import lax
from jax.experimental import pallas as pl
from jax.experimental.pallas import tpu as pltpu
from jax.sharding import PartitionSpec as P

WIDTH = 64
REB = 2
EPSILON = 1e-05
F32 = jnp.float32
BF16 = jnp.bfloat16
HIGH = lax.Precision.HIGHEST
VMEM_LIMIT = 40 * 1024 * 1024
SMEM_SPEC = pl.BlockSpec(memory_space=pltpu.SMEM)
VMEM_SPEC = pl.BlockSpec(memory_space=pltpu.VMEM)
ANY_SPEC = pl.BlockSpec(memory_space=pl.ANY)


def rotate(value, axis, steps):
    count = lax.axis_size(axis)
    pairs = [(source, (source + steps) % count) for source in range(count)]
    return lax.ppermute(value, axis, pairs)


def on_chip(value):
    return pltpu.with_memory_space_constraint(value, pltpu.VMEM)


def call(kernel, name, out_shape, operands, scratch=()):
    specs = {"smem": SMEM_SPEC, "vmem": VMEM_SPEC, "any": ANY_SPEC}
    return pl.pallas_call(
        kernel,
        name=name,
        out_shape=out_shape,
        in_specs=[specs[place] for _, place in operands],
        out_specs=jax.tree.map(lambda _: VMEM_SPEC, out_shape),
        scratch_shapes=list(scratch),
        compiler_params=pltpu.CompilerParams(vmem_limit_bytes=VMEM_LIMIT),
    )(*[on_chip(array) if place == "vmem" else array for array, place in operands])


def out(shape, dtype):
    return jax.ShapeDtypeStruct(shape, dtype)


def normalize(rows, gain):
    centered = rows - jnp.mean(rows, axis=-1, keepdims=True)
    spread = jnp.mean(centered * centered, axis=-1, keepdims=True)
    return (centered * lax.rsqrt(spread + EPSILON) * gain).astype(BF16).astype(F32)


def dot(left, right, contract=(1, 0), precision=None):
    return lax.dot_general(
        left,
        right,
        (((contract[0],), (contract[1],)), ((), ())),
        precision=precision,
        preferred_element_type=F32,
    )


def halves(value):
    high = value.astype(BF16)
    return high, (value - high.astype(F32)).astype(BF16)


def iota(shape, axis):
    return lax.broadcasted_iota(jnp.int32, shape, axis)


def column_of(scalars, rows, lanes):
    row = iota((rows, lanes), 0)
    result = jnp.zeros((rows, lanes), jnp.int32)
    for index in range(rows):
        result = jnp.where(row == index, scalars[index], result)
    return result


def head_blocks(lanes):
    return iota((lanes, lanes), 0) // WIDTH == iota((lanes, lanes), 1) // WIDTH


def head_sums(rows):
    ones = head_blocks(rows.shape[1]).astype(BF16)
    high, low = halves(rows)
    return dot(high, ones) + dot(low, ones)


def pack_kernel(former, marks, held, state, shifts, tokens, gathered, chain_a, chain_b, part, sems):
    count = state.shape[0]
    heads = state.shape[1]
    hist = held.shape[1]
    quarter = heads * WIDTH
    rank = jnp.int32(0)
    chosen = [jnp.int32(0)] * REB
    for index in range(count):
        marked = marks[index] == 1
        chosen = [
            jnp.where(marked & (rank == place), index, value) for place, value in enumerate(chosen)
        ]
        rank = rank + marks[index]
    copies = [
        pltpu.make_async_copy(held.at[value], gathered.at[pl.ds(place * hist, hist)], sems.at[place])
        for place, value in enumerate(chosen)
    ]
    for copy in copies:
        copy.start()
    half = count // 2
    for chain, target in enumerate((chain_a, chain_b)):
        part[...] = jnp.zeros_like(part)
        for index in range(half):
            source = lax.rem(former[chain * half + index], count)
            whole = state[source]
            packed = jnp.concatenate([whole[head] for head in range(heads)], axis=1)
            target[pl.ds(index * WIDTH, WIDTH), :] = packed.astype(BF16)
            line = shifts[source]
            for piece in range(4):
                which, lane = piece // 2, (piece % 2) * quarter
                part[piece * half + index : piece * half + index + 1, :] = line[
                    which : which + 1, lane : lane + quarter
                ]
        target[pl.ds(half * WIDTH, 4 * half), :] = part[...].astype(BF16)
    gathered[pl.ds(REB * hist, tokens.shape[0]), :] = tokens[...]
    for copy in copies:
        copy.wait()


def project_kernel(
    head, occupied, own, by_one, by_two, by_three, gain, rates, w_r, w_k, w_v, w_left, w_right, base,
    a_r, a_k, a_v, a_l, rebuilt, last_hist, time_last,
    entries,
):
    ranks = 4
    feature = own.shape[1]
    hist_rows = REB * 32
    tokens = own.shape[0] - hist_rows
    count = tokens // 4
    me = head[0]
    for steps, piece in enumerate((own, by_one, by_two, by_three)):
        block = lax.rem(me - steps + ranks, ranks)
        entries[:, pl.ds(pl.multiple_of(block * feature, feature), feature)] = piece[...].astype(F32)
    current = normalize(entries[...], gain[...])
    hist = current[:hist_rows]
    live = current[hist_rows:]
    place = iota(hist.shape, 0) % 32
    hist_previous = jnp.where(place == 0, 0.0, pltpu.roll(hist, 1, 0))
    live_previous = jnp.concatenate([jnp.zeros_like(live[:count]), live[:-count]], axis=0)
    previous = jnp.concatenate([hist_previous, live_previous], axis=0)
    change = previous - current

    def mixed(which):
        return (current + change * rates[which : which + 1, :]).astype(BF16)

    a_r[...] = dot(mixed(0)[hist_rows:], w_r[...])
    keys = dot(mixed(1), w_k[...])
    values = dot(mixed(2), w_v[...])
    low = dot(mixed(3), w_left[...], (1, 1))
    a_k[...] = keys[hist_rows:]
    a_v[...] = values[hist_rows:]
    a_l[...] = low[hist_rows:]
    keys, values, low = keys[:hist_rows], values[:hist_rows], low[:hist_rows]
    rank = jnp.tanh(low).astype(BF16)
    decay = jnp.exp(-jnp.exp(base[...] + dot(rank, w_right[...])))
    spot = iota(decay.shape, 0) % 32
    product = decay
    for steps in (1, 2, 4, 8, 16):
        product = product * jnp.where(spot + steps < 32, pltpu.roll(product, hist_rows - steps, 0), 1.0)
    later = jnp.where(spot < 31, pltpu.roll(product, hist_rows - 1, 0), 1.0)
    keys = keys * later
    lane = iota((WIDTH, values.shape[1]), 1) // WIDTH
    for slot in range(REB):
        span = slice(slot * 32, slot * 32 + 32)
        k_high, k_low = halves(keys[span])
        v_high, v_low = halves(values[span])
        outer = dot(
            jnp.concatenate([k_high, k_high, k_low], axis=0),
            jnp.concatenate([v_high, v_low, v_high], axis=0),
            (0, 0),
        )
        packed = outer[:WIDTH]
        for which in range(1, values.shape[1] // WIDTH):
            packed = jnp.where(lane == which, outer[which * WIDTH : (which + 1) * WIDTH], packed)
        rebuilt[slot] = packed
        last_hist[slot : slot + 1, :] = hist[slot * 32 + 31 : slot * 32 + 32]
    occ = column_of(occupied, count, current.shape[1])
    last = jnp.zeros((count, current.shape[1]), F32)
    for slot in range(4):
        last = jnp.where(occ == slot + 1, live[slot * count : (slot + 1) * count], last)
    entries[pl.ds(0, count), :] = last
    time_last[...] = entries[pl.ds(0, count), pl.ds(pl.multiple_of(me * feature, feature), feature)]


def recur_kernel(
    head, occupied, marks, chain_a, chain_b, own, by_one, by_two, by_three, last_hist, rebuilt,
    a_r, a_k, a_v, a_l, rates, w_r, w_k, w_v, w_left, w_right, base, reward, gain, w_out,
    next_state, partial, shift_ffn,
    start_shift,
):
    ranks = 4
    count = marks.shape[0]
    half = count // 2
    quarter = own.shape[1]
    channels = a_r.shape[1]
    me = head[0]
    for steps, piece in enumerate((own, by_one, by_two, by_three)):
        block = lax.rem(me - steps + ranks, ranks)
        lines = piece[...].astype(F32)
        for chain in range(2):
            for part in range(4):
                target = start_shift if part < 2 else shift_ffn
                lane = pl.multiple_of(block * (2 * quarter) + (part % 2) * quarter, quarter)
                row = chain * 4 * half + part * half
                target[pl.ds(chain * half, half), pl.ds(lane, quarter)] = lines[row : row + half]
    rank = jnp.int32(0)
    place = []
    for index in range(count):
        place.append(jnp.where(marks[index] == 1, rank, REB))
        rank = rank + marks[index]
    slots = column_of(place, count, start_shift.shape[1])
    start = start_shift[...]
    for slot in range(REB):
        start = jnp.where(slots == slot, last_hist[slot : slot + 1, :], start)

    def first(which):
        return (start * rates[which : which + 1, :]).astype(BF16)

    def with_first(rows, extra):
        return jnp.concatenate([rows[:count] + extra, rows[count:]], axis=0)

    received = with_first(a_r[...], dot(first(0), w_r[...]))
    keys = with_first(a_k[...], dot(first(1), w_k[...]))
    values = with_first(a_v[...], dot(first(2), w_v[...]))
    low = jnp.tanh(with_first(a_l[...], dot(first(3), w_left[...], (1, 1)))).astype(BF16)
    decay = jnp.exp(-jnp.exp(base[...] + dot(low, w_right[...])))
    occ = column_of(occupied, count, channels)
    slot_of = lambda rows: [rows[slot * count : (slot + 1) * count] for slot in range(4)]
    r, k, v, d = slot_of(received), slot_of(keys), slot_of(values), slot_of(decay)
    d = [jnp.where(occ > slot, d[slot], 1.0) for slot in range(4)]
    k_live = [jnp.where(occ > slot, k[slot], 0.0) for slot in range(4)]
    before = [jnp.ones_like(d[0])]
    for slot in range(4):
        before.append(before[-1] * d[slot])
    query = jnp.concatenate([r[slot] * before[slot] for slot in range(4)], axis=0)
    scores, pairs = [], []
    for slot in range(4):
        scores.append(r[slot] * reward[...] * k[slot])
        pairs.append((slot, slot))
        between = jnp.ones_like(d[0])
        for earlier in range(slot - 1, -1, -1):
            scores.append(r[slot] * between * k_live[earlier])
            pairs.append((slot, earlier))
            between = between * d[earlier]
    sums = head_sums(jnp.concatenate(scores, axis=0))
    inner = [jnp.zeros_like(v[0])] * 4
    for index, (slot, earlier) in enumerate(pairs):
        inner[slot] = inner[slot] + sums[index * count : (index + 1) * count] * v[earlier]
    mixed = jnp.concatenate(inner, axis=0)
    after = jnp.ones_like(d[0])
    k_after = [None] * 4
    for slot in range(3, -1, -1):
        k_after[slot] = k_live[slot] * after
        after = after * d[slot]
    k_high, k_low = halves(jnp.concatenate(k_after, axis=0))
    v_high, v_low = halves(values)
    k_rows = jnp.concatenate([k_high, k_high, k_low], axis=0)
    v_rows = jnp.concatenate([v_high, v_low, v_high], axis=0).astype(F32)
    k_columns = jnp.transpose(k_rows.astype(F32)).astype(BF16)
    after_columns = jnp.transpose(before[4])
    q_high, q_low = halves(query)
    q_rows = jnp.concatenate([q_high, q_low], axis=0).astype(F32)
    q_request = iota(q_rows.shape, 0) % count
    v_request = iota(v_rows.shape, 0) % count
    blocks = head_blocks(channels)
    total = jnp.zeros((q_rows.shape[0], channels), F32)
    for index in range(count):
        chain = chain_a if index < half else chain_b
        packed = chain[pl.ds((index % half) * WIDTH, WIDTH), :].astype(F32)
        for slot in range(REB):
            packed = jnp.where(place[index] == slot, rebuilt[slot], packed)
        tall = jnp.concatenate([packed] * (channels // WIDTH), axis=0)
        tall = jnp.where(blocks, tall, 0.0).astype(BF16)
        total = total + dot(jnp.where(q_request == index, q_rows, 0.0).astype(BF16), tall)
        update = dot(k_columns, jnp.where(v_request == index, v_rows, 0.0).astype(BF16))
        for which in range(channels // WIDTH):
            rows = slice(which * WIDTH, (which + 1) * WIDTH)
            lanes = slice(which // 2 * 128, which // 2 * 128 + 128)
            block = update[rows, lanes] + after_columns[rows, index : index + 1] * packed[:, lanes]
            if which % 2:
                block = pltpu.roll(block, 64, 1)
            next_state[index, which] = block[:, :WIDTH]
    mixed = mixed + total[: 4 * count] + total[4 * count :]
    centered = mixed - head_sums(mixed) * (1.0 / WIDTH)
    spread = head_sums(centered * centered) * (1.0 / WIDTH)
    heads_out = (centered * lax.rsqrt(spread + EPSILON) * gain[...]).astype(BF16)
    partial[...] = dot(heads_out, w_out[...]).astype(BF16)


def ffn_kernel(
    head, occupied, own, by_one, by_two, by_three, p_own, p_one, p_two, p_three, shift_ffn, gain, rates,
    w_up, w_down,
    kept, to_one, to_two, to_three, channel_last,
    entries,
):
    ranks = 4
    feature = own.shape[1]
    tokens = p_own.shape[0]
    count = tokens // 4
    hist_rows = own.shape[0] - tokens
    me = head[0]
    for steps, piece in enumerate((own, by_one, by_two, by_three)):
        block = lax.rem(me - steps + ranks, ranks)
        entries[:, pl.ds(pl.multiple_of(block * feature, feature), feature)] = piece[
            pl.ds(hist_rows, tokens), :
        ].astype(F32)
    mix = sum(piece[...].astype(F32) for piece in (p_own, p_one, p_two, p_three))
    middle = (entries[...] + mix).astype(BF16).astype(F32)
    entries[...] = middle
    own_lanes = pl.ds(pl.multiple_of(me * feature, feature), feature)
    middle_own = entries[:, own_lanes]
    current = normalize(middle, gain[...])
    previous = jnp.concatenate([shift_ffn[...], current[:-count]], axis=0)
    blended = (current + (previous - current) * rates[4:5, :]).astype(BF16)
    hidden = jnp.maximum(dot(blended, w_up[...]), 0.0)
    hidden = (hidden * hidden).astype(BF16)
    for steps, target in enumerate((kept, to_one, to_two, to_three)):
        block = lax.rem(me + steps, ranks)
        lanes = pl.ds(pl.multiple_of(block * feature, feature), feature)
        rows = dot(hidden, w_down[:, lanes])
        if steps == 0:
            target[...] = rows + middle_own
        else:
            target[...] = rows.astype(BF16)
    occ = column_of(occupied, count, current.shape[1])
    last = jnp.zeros((count, current.shape[1]), F32)
    for slot in range(4):
        last = jnp.where(occ == slot + 1, current[slot * count : (slot + 1) * count], last)
    entries[pl.ds(0, count), :] = last
    channel_last[...] = entries[pl.ds(0, count), own_lanes]


def on_device(
    arriving_hiddens,
    occupied_slot_totals,
    former_indices,
    reconstruct_marks,
    retained_hiddens,
    carried_memory_matrices,
    lagged_previous_entries,
    pre_attention_scaling,
    pre_feedforward_scaling,
    lag_blend_fractions,
    acceptance_projection,
    address_projection,
    content_projection,
    fading_lowrank_left,
    fading_lowrank_right,
    fading_baseline_entries,
    present_item_reward,
    grouped_layer_scaling,
    attention_exit_projection,
    feedforward_address_proj,
    feedforward_content_proj,
):
    count, steps, feature = arriving_hiddens.shape
    half = count // 2
    heads = carried_memory_matrices.shape[1]
    channels = heads * WIDTH
    hist = retained_hiddens.shape[1]
    model = pre_attention_scaling.shape[0]
    tokens = count * steps
    groups = lax.axis_size("grp")
    head = lax.axis_index("head").astype(jnp.int32).reshape(1)
    row = lambda value: value.reshape(1, -1)
    token_rows = jnp.swapaxes(arriving_hiddens, 0, 1).reshape(tokens, feature)
    chain_rows = half * WIDTH + 4 * half
    gathered, chain_a, chain_b = call(
        pack_kernel,
        "pack",
        (
            out((REB * hist + tokens, feature), BF16),
            out((chain_rows, channels), BF16),
            out((chain_rows, channels), BF16),
        ),
        [
            (former_indices, "smem"),
            (reconstruct_marks, "smem"),
            (retained_hiddens, "any"),
            (carried_memory_matrices, "vmem"),
            (lagged_previous_entries, "vmem"),
            (token_rows, "vmem"),
        ],
        [pltpu.VMEM((4 * half, channels), F32), pltpu.SemaphoreType.DMA((REB,))],
    )
    grp_index = lax.axis_index("grp")
    offset = (former_indices // count - grp_index) % groups
    request = jnp.where(
        jnp.arange(chain_rows) < half * WIDTH, jnp.arange(chain_rows) // WIDTH, jnp.arange(chain_rows) % half
    )
    member = request[:, None] == jnp.arange(half)[None, :]
    row_offset_a = jnp.sum(jnp.where(member, offset[None, :half], 0), axis=1, keepdims=True)
    row_offset_b = jnp.sum(jnp.where(member, (groups - offset[None, half:]) % groups, 0), axis=1, keepdims=True)
    pieces = [gathered] + [rotate(gathered, "head", k) for k in (1, 3, 2)]
    pieces = [pieces[0], pieces[1], pieces[3], pieces[2]]
    for bit in range((groups - 1).bit_length()):
        moved_a = rotate(chain_a, "grp", -(1 << bit))
        moved_b = rotate(chain_b, "grp", 1 << bit)
        chain_a = jnp.where(row_offset_a >> bit & 1 == 1, moved_a, chain_a)
        chain_b = jnp.where(row_offset_b >> bit & 1 == 1, moved_b, chain_b)
    attention_gain = row(pre_attention_scaling)
    base = row(fading_baseline_entries)
    left = fading_lowrank_left.T
    a_r, a_k, a_v, a_l, rebuilt, last_hist, time_last = call(
        project_kernel,
        "project",
        (
            out((tokens, channels), F32),
            out((tokens, channels), F32),
            out((tokens, channels), F32),
            out((tokens, left.shape[0]), F32),
            out((REB, WIDTH, channels), F32),
            out((REB, model), F32),
            out((count, feature), F32),
        ),
        [(head, "smem"), (occupied_slot_totals, "smem")]
        + [
            (value, "vmem")
            for value in (
                *pieces,
                attention_gain,
                lag_blend_fractions,
                acceptance_projection,
                address_projection,
                content_projection,
                left,
                fading_lowrank_right,
                base,
            )
        ],
        [pltpu.VMEM((REB * hist + tokens, model), F32)],
    )
    shift_rows = jnp.concatenate([chain_a[half * WIDTH :], chain_b[half * WIDTH :]], axis=0)
    shift_pieces = [shift_rows] + [rotate(shift_rows, "head", k) for k in (1, 2, 3)]
    next_state, partial, shift_ffn = call(
        recur_kernel,
        "recur",
        (
            out((count, heads, WIDTH, WIDTH), F32),
            out((tokens, model), BF16),
            out((count, model), F32),
        ),
        [(head, "smem"), (occupied_slot_totals, "smem"), (reconstruct_marks, "smem")]
        + [
            (value, "vmem")
            for value in (
                chain_a,
                chain_b,
                *shift_pieces,
                last_hist,
                rebuilt,
                a_r,
                a_k,
                a_v,
                a_l,
                lag_blend_fractions,
                acceptance_projection,
                address_projection,
                content_projection,
                left,
                fading_lowrank_right,
                base,
                row(present_item_reward),
                row(grouped_layer_scaling),
                attention_exit_projection,
            )
        ],
        [pltpu.VMEM((count, model), F32)],
    )
    partials = [partial] + [rotate(partial, "head", k) for k in (1, 2, 3)]
    kept, to_one, to_two, to_three, channel_last = call(
        ffn_kernel,
        "ffn",
        (
            out((tokens, feature), F32),
            out((tokens, feature), BF16),
            out((tokens, feature), BF16),
            out((tokens, feature), BF16),
            out((count, feature), F32),
        ),
        [(head, "smem"), (occupied_slot_totals, "smem")]
        + [
            (value, "vmem")
            for value in (
                *pieces,
                *partials,
                shift_ffn,
                row(pre_feedforward_scaling),
                lag_blend_fractions,
                feedforward_address_proj,
                feedforward_content_proj,
            )
        ],
        [pltpu.VMEM((tokens, model), F32)],
    )
    arrived = [rotate(value, "head", k + 1) for k, value in enumerate((to_one, to_two, to_three))]
    result = kept + sum(value.astype(F32) for value in arrived)
    result = jnp.swapaxes(result.astype(BF16).reshape(steps, count, feature), 0, 1)
    valid_rows = jnp.arange(steps)[None, :] < occupied_slot_totals[:, None]
    result = jnp.where(valid_rows[..., None], result, jnp.zeros_like(result))
    return (result, next_state, jnp.stack([time_last, channel_last], axis=1))


def solution(mesh):
    placed = (
        P("grp", None, "head"),
        P("grp"),
        P("grp"),
        P("grp"),
        P("grp", None, "head"),
        P("grp", "head", None, None),
        P("grp", None, "head"),
        P(),
        P(),
        P(),
        P(None, "head"),
        P(None, "head"),
        P(None, "head"),
        P(),
        P(None, "head"),
        P("head"),
        P("head"),
        P("head"),
        P("head", None),
        P(None, "head"),
        P("head", None),
    )
    return jax.shard_map(
        on_device,
        mesh=mesh,
        in_specs=placed,
        out_specs=(P("grp", None, "head"), P("grp", "head", None, None), P("grp", None, "head")),
        check_vma=False,
    )
```

```python
import functools

import jax
import jax.numpy as jnp
from jax import lax
from jax.experimental import pallas as pl
from jax.experimental.pallas import tpu as pltpu
from jax.sharding import PartitionSpec as P

WIDTH = 64
REB = 2
EPSILON = 1e-05
F32 = jnp.float32
BF16 = jnp.bfloat16
HIGH = lax.Precision.HIGHEST
VMEM_LIMIT = 40 * 1024 * 1024
SMEM_SPEC = pl.BlockSpec(memory_space=pltpu.SMEM)
VMEM_SPEC = pl.BlockSpec(memory_space=pltpu.VMEM)
ANY_SPEC = pl.BlockSpec(memory_space=pl.ANY)


def rotate(value, axis, steps):
    count = lax.axis_size(axis)
    pairs = [(source, (source + steps) % count) for source in range(count)]
    return lax.ppermute(value, axis, pairs)


def on_chip(value):
    return pltpu.with_memory_space_constraint(value, pltpu.VMEM)


def off_chip(value):
    return pltpu.with_memory_space_constraint(value, pltpu.HBM)


SPECS = {"smem": SMEM_SPEC, "vmem": VMEM_SPEC, "load": VMEM_SPEC, "any": ANY_SPEC, "scalars": SMEM_SPEC}
PLACES = {"vmem": on_chip, "load": off_chip, "any": off_chip, "scalars": off_chip}


def call(kernel, name, out_shape, operands, scratch=(), out_specs=None):
    return pl.pallas_call(
        kernel,
        name=name,
        out_shape=out_shape,
        in_specs=[SPECS[place] for _, place in operands],
        out_specs=jax.tree.map(lambda _: VMEM_SPEC, out_shape) if out_specs is None else out_specs,
        scratch_shapes=list(scratch),
        compiler_params=pltpu.CompilerParams(vmem_limit_bytes=VMEM_LIMIT),
    )(*[PLACES.get(place, lambda value: value)(array) for array, place in operands])


def out(shape, dtype):
    return jax.ShapeDtypeStruct(shape, dtype)


def normalize(rows, gain):
    centered = rows - jnp.mean(rows, axis=-1, keepdims=True)
    spread = jnp.mean(centered * centered, axis=-1, keepdims=True)
    return (centered * lax.rsqrt(spread + EPSILON) * gain).astype(BF16).astype(F32)


def dot(left, right, contract=(1, 0), precision=None):
    return lax.dot_general(
        left,
        right,
        (((contract[0],), (contract[1],)), ((), ())),
        precision=precision,
        preferred_element_type=F32,
    )


def halves(value):
    high = value.astype(BF16)
    return high, (value - high.astype(F32)).astype(BF16)


def iota(shape, axis):
    return lax.broadcasted_iota(jnp.int32, shape, axis)


def column_of(plan, base, rows, lanes):
    row = iota((rows, lanes), 0)
    result = jnp.zeros((rows, lanes), jnp.int32)
    for index in range(rows):
        result = jnp.where(row == index, plan[base + index], result)
    return result


def head_blocks(lanes):
    return iota((lanes, lanes), 0) // WIDTH == iota((lanes, lanes), 1) // WIDTH


def head_sums(rows):
    ones = head_blocks(rows.shape[1]).astype(BF16)
    high, low = halves(rows)
    return dot(high, ones) + dot(low, ones)


STRIDES = (24, 3, 8, 1)
DIGIT, PLACE, OCCUPIED, PLAN = 0, 32, 40, 48
AUX = 7


def pack_kernel(
    former, marks, occupied, held, state, shifts, tokens,
    gathered, packed, plan,
    slots, rows, sems, row_sems,
):
    count, heads = rows.shape[0], rows.shape[1]
    hist = held.shape[1]
    groups = lax.axis_size("grp")
    here = lax.axis_index("grp")
    sources = [lax.rem(former[index], count) for index in range(count)]
    row_copies = [
        pltpu.make_async_copy(state.at[source], rows.at[index], row_sems.at[index])
        for index, source in enumerate(sources)
    ]
    for copy in row_copies:
        copy.start()
    rank = jnp.int32(0)
    chosen = [jnp.int32(0)] * REB
    for index in range(count):
        marked = marks[index] == 1
        chosen = [
            jnp.where(marked & (rank == place), index, value) for place, value in enumerate(chosen)
        ]
        plan[PLACE + index] = jnp.where(marked, rank, REB)
        rank = rank + marks[index]
        plan[OCCUPIED + index] = occupied[index]
    copies = [
        pltpu.make_async_copy(held.at[value], gathered.at[pl.ds(place * hist, hist)], sems.at[place])
        for place, value in enumerate(chosen)
    ]
    for copy in copies:
        copy.start()
    for index in range(count):
        distance = lax.rem(former[index] // count - here + groups, groups)
        low = lax.rem(distance, 8)
        low = jnp.where(low > 4, low - 8, low)
        high = lax.rem(lax.div(distance - low + groups, 8), 8)
        high = jnp.where(high > 4, high - 8, high)
        for far, near, value in ((0, 2, high), (1, 3, low)):
            triple = jnp.where(value >= 2, 1, jnp.where(value <= -2, -1, 0))
            plan[DIGIT + far * count + index] = triple
            plan[DIGIT + near * count + index] = value - 3 * triple
    base = REB * hist
    for index in range(count):
        lines = tokens[index].astype(F32)
        for slot in range(4):
            slots[slot * count + index : slot * count + index + 1, :] = lines[slot : slot + 1]
        line = shifts[sources[index]]
        for which in range(2):
            row = (4 + which) * count + index
            slots[row : row + 1, :] = line[which : which + 1]
    gathered[pl.ds(base, slots.shape[0]), :] = slots[...].astype(BF16)
    for index in range(count):
        row_copies[index].wait()
        whole = rows[index]
        wide = jnp.concatenate([whole[head] for head in range(heads)], axis=1)
        packed[pl.ds(index * WIDTH, WIDTH), :] = wide.astype(BF16)
    for copy in copies:
        copy.wait()


def digits_of(plan, stage, count):
    return [plan[DIGIT + stage * count + index] for index in range(count)]


def pick_rows(digits, plus, minus, stay, merged, count):
    for index, digit in enumerate(digits):
        rows = pl.ds(index * WIDTH, WIDTH)
        for value, source in ((1, plus), (-1, minus), (0, stay)):

            @pl.when(digit == value)
            def _(rows=rows, source=source):
                merged[rows, :] = source[rows, :]


def pick_aux(digits, plus, minus, stay, count):
    shape = (count, plus.shape[1])
    request = iota(shape, 0)
    take = jnp.zeros(shape, jnp.int32)
    for index, digit in enumerate(digits):
        take = jnp.where(request == index, digit, take)
    take = jnp.concatenate([take] * (plus.shape[0] // count), axis=0)
    plus, minus, stay = (value.astype(F32) for value in (plus, minus, stay))
    return jnp.where(take == 1, plus, jnp.where(take == -1, minus, stay))


def merge_first_kernel(plan, plus, minus, stay, aux_plus, aux_minus, aux_stay, merged):
    count = plus.shape[0] // WIDTH
    digits = digits_of(plan, 0, count)
    pick_rows(digits, plus, minus, stay, merged, count)
    picked = pick_aux(digits, aux_plus[...], aux_minus[...], aux_stay[...], count)
    merged[pl.ds(count * WIDTH, AUX * count), :] = picked.astype(BF16)


def merge_kernel(stage, plan, plus, minus, stay, merged):
    count = plus.shape[0] // (WIDTH + AUX)
    digits = digits_of(plan, stage, count)
    pick_rows(digits, plus, minus, stay, merged, count)
    tail = pl.ds(count * WIDTH, AUX * count)
    picked = pick_aux(digits, plus[tail, :], minus[tail, :], stay[tail, :], count)
    merged[tail, :] = picked.astype(BF16)


def project_kernel(
    plan, own, by_one, by_two, by_three, gain, rates, far_r, far_k, far_v, far_left, far_up, w_right, base,
    a_r, a_k, a_v, a_l, rebuilt, aux, hist_first, hist_low, time_last,
    entries, w_r, w_k, w_v, w_left, w_up, sems,
):
    copies = [
        pltpu.make_async_copy(far, near, sems.at[index])
        for index, (far, near) in enumerate(
            ((far_k, w_k), (far_v, w_v), (far_left, w_left), (far_r, w_r), (far_up, w_up))
        )
    ]
    for copy in copies:
        copy.start()
    ranks = 4
    feature = own.shape[1]
    hist_rows = REB * 32
    tokens = a_r.shape[0]
    count = tokens // 4
    normal = hist_rows + tokens
    me = lax.axis_index("head")
    for steps, piece in enumerate((own, by_one, by_two, by_three)):
        block = lax.rem(me - steps + ranks, ranks)
        entries[:, pl.ds(pl.multiple_of(block * feature, feature), feature)] = piece[...].astype(F32)
    current = normalize(entries[pl.ds(0, normal), :], gain[...])
    hist = current[:hist_rows]
    live = current[hist_rows:]
    place = iota(hist.shape, 0) % 32
    hist_previous = jnp.where(place == 0, 0.0, pltpu.roll(hist, 1, 0))
    live_previous = jnp.concatenate([jnp.zeros_like(live[:count]), live[:-count]], axis=0)
    previous = jnp.concatenate([hist_previous, live_previous], axis=0)
    change = previous - current
    moved_shift = entries[pl.ds(normal, count), :]
    lines = iota(moved_shift.shape, 0)
    last_hist = jnp.zeros_like(moved_shift)
    for slot in range(REB):
        last_hist = jnp.where(lines == slot, hist[slot * 32 + 31 : slot * 32 + 32], last_hist)
    first = jnp.concatenate([moved_shift, last_hist], axis=0)

    def mixed(which):
        rate = rates[which : which + 1, :]
        return jnp.concatenate([current + change * rate, first * rate], axis=0).astype(BF16)

    copies[0].wait()
    keys = dot(mixed(1), w_k[...])
    copies[1].wait()
    values = dot(mixed(2), w_v[...])
    copies[2].wait()
    low = dot(mixed(3), w_left[...], (1, 1))
    copies[3].wait()
    received = dot(mixed(0)[hist_rows:], w_r[...])
    a_r[...] = received[:tokens]
    a_k[...] = keys[hist_rows:normal]
    a_v[...] = values[hist_rows:normal]
    a_l[...] = low[hist_rows:normal]
    hist_first[0] = received[tokens + count :]
    hist_first[1] = keys[normal + count :]
    hist_first[2] = values[normal + count :]
    hist_low[...] = low[normal + count :]
    copies[4].wait()
    up = dot((entries[pl.ds(normal + count, count), :] * rates[4:5, :]).astype(BF16), w_up[...])
    lanes = aux.shape[1]
    whole = up.shape[1] // lanes
    left = jnp.concatenate([low[normal : normal + count], jnp.zeros((count, lanes // 2 - low.shape[1]), F32)], axis=1)
    moving = [received[tokens : tokens + count], keys[normal : normal + count], values[normal : normal + count]]
    moving += [up[:, part * lanes : (part + 1) * lanes] for part in range(whole)]
    moving += [jnp.concatenate([left, up[:, whole * lanes :]], axis=1)]
    aux[...] = jnp.concatenate(moving, axis=0).astype(BF16)
    keys, values, low = keys[:hist_rows], values[:hist_rows], low[:hist_rows]
    rank = jnp.tanh(low).astype(BF16)
    decay = jnp.exp(-jnp.exp(base[...] + dot(rank, w_right[...])))
    spot = iota(decay.shape, 0) % 32
    product = decay
    for steps in (1, 2, 4, 8, 16):
        product = product * jnp.where(spot + steps < 32, pltpu.roll(product, hist_rows - steps, 0), 1.0)
    later = jnp.where(spot < 31, pltpu.roll(product, hist_rows - 1, 0), 1.0)
    keys = keys * later
    lane = iota((WIDTH, values.shape[1]), 1) // WIDTH
    for slot in range(REB):
        span = slice(slot * 32, slot * 32 + 32)
        k_high, k_low = halves(keys[span])
        v_high, v_low = halves(values[span])
        outer = dot(
            jnp.concatenate([k_high, k_high, k_low], axis=0),
            jnp.concatenate([v_high, v_low, v_high], axis=0),
            (0, 0),
        )
        packed = outer[:WIDTH]
        for which in range(1, values.shape[1] // WIDTH):
            packed = jnp.where(lane == which, outer[which * WIDTH : (which + 1) * WIDTH], packed)
        rebuilt[slot] = packed
    occ = column_of(plan, OCCUPIED, count, current.shape[1])
    last = jnp.zeros((count, current.shape[1]), F32)
    for slot in range(4):
        last = jnp.where(occ == slot + 1, live[slot * count : (slot + 1) * count], last)
    entries[pl.ds(0, count), :] = last
    time_last[...] = entries[pl.ds(0, count), pl.ds(pl.multiple_of(me * feature, feature), feature)]


def recur_kernel(
    plan, moved, hist_first, hist_low, rebuilt, a_r, a_k, a_v, a_l, w_right, base, reward, gain, w_out,
    next_state, partial, up_first,
):
    count = next_state.shape[0]
    channels = a_r.shape[1]
    place = [plan[PLACE + index] for index in range(count)]
    slots = column_of(plan, PLACE, count, channels)
    aux = moved[pl.ds(count * WIDTH, AUX * count), :].astype(F32)
    block = lambda part: aux[part * count : (part + 1) * count]
    inner = hist_low.shape[1]

    def with_first(rows, extra, hist):
        for slot in range(REB):
            extra = jnp.where(slots[:, : extra.shape[1]] == slot, hist[slot : slot + 1, :], extra)
        return jnp.concatenate([rows[:count] + extra, rows[count:]], axis=0)

    received = with_first(a_r[...], block(0), hist_first[0])
    keys = with_first(a_k[...], block(1), hist_first[1])
    values = with_first(a_v[...], block(2), hist_first[2])
    low = jnp.tanh(with_first(a_l[...], block(6)[:, :inner], hist_low[...])).astype(BF16)
    up_first[...] = jnp.concatenate([block(3), block(4), block(5), block(6)[:, channels // 2 :]], axis=1)
    decay = jnp.exp(-jnp.exp(base[...] + dot(low, w_right[...])))
    occ = column_of(plan, OCCUPIED, count, channels)
    slot_of = lambda rows: [rows[slot * count : (slot + 1) * count] for slot in range(4)]
    r, k, v, d = slot_of(received), slot_of(keys), slot_of(values), slot_of(decay)
    d = [jnp.where(occ > slot, d[slot], 1.0) for slot in range(4)]
    k_live = [jnp.where(occ > slot, k[slot], 0.0) for slot in range(4)]
    before = [jnp.ones_like(d[0])]
    for slot in range(4):
        before.append(before[-1] * d[slot])
    query = jnp.concatenate([r[slot] * before[slot] for slot in range(4)], axis=0)
    scores, pairs = [], []
    for slot in range(4):
        scores.append(r[slot] * reward[...] * k[slot])
        pairs.append((slot, slot))
        between = jnp.ones_like(d[0])
        for earlier in range(slot - 1, -1, -1):
            scores.append(r[slot] * between * k_live[earlier])
            pairs.append((slot, earlier))
            between = between * d[earlier]
    sums = head_sums(jnp.concatenate(scores, axis=0))
    inner = [jnp.zeros_like(v[0])] * 4
    for index, (slot, earlier) in enumerate(pairs):
        inner[slot] = inner[slot] + sums[index * count : (index + 1) * count] * v[earlier]
    mixed = jnp.concatenate(inner, axis=0)
    after = jnp.ones_like(d[0])
    k_after = [None] * 4
    for slot in range(3, -1, -1):
        k_after[slot] = k_live[slot] * after
        after = after * d[slot]
    k_high, k_low = halves(jnp.concatenate(k_after, axis=0))
    v_high, v_low = halves(values)
    k_rows = jnp.concatenate([k_high, k_high, k_low], axis=0)
    v_rows = jnp.concatenate([v_high, v_low, v_high], axis=0).astype(F32)
    k_columns = jnp.transpose(k_rows.astype(F32)).astype(BF16)
    after_columns = jnp.transpose(before[4])
    q_high, q_low = halves(query)
    q_rows = jnp.concatenate([q_high, q_low], axis=0).astype(F32)
    q_request = iota(q_rows.shape, 0) % count
    v_request = iota(v_rows.shape, 0) % count
    blocks = head_blocks(channels)
    total = jnp.zeros((q_rows.shape[0], channels), F32)
    for index in range(count):
        packed = moved[pl.ds(index * WIDTH, WIDTH), :].astype(F32)
        for slot in range(REB):
            packed = jnp.where(place[index] == slot, rebuilt[slot], packed)
        tall = jnp.concatenate([packed] * (channels // WIDTH), axis=0)
        tall = jnp.where(blocks, tall, 0.0).astype(BF16)
        total = total + dot(jnp.where(q_request == index, q_rows, 0.0).astype(BF16), tall)
        update = dot(k_columns, jnp.where(v_request == index, v_rows, 0.0).astype(BF16))
        for which in range(channels // WIDTH):
            rows = slice(which * WIDTH, (which + 1) * WIDTH)
            lanes = slice(which // 2 * 128, which // 2 * 128 + 128)
            block = update[rows, lanes] + after_columns[rows, index : index + 1] * packed[:, lanes]
            if which % 2:
                block = pltpu.roll(block, 64, 1)
            next_state[index, which] = block[:, :WIDTH]
    mixed = mixed + total[: 4 * count] + total[4 * count :]
    centered = mixed - head_sums(mixed) * (1.0 / WIDTH)
    spread = head_sums(centered * centered) * (1.0 / WIDTH)
    heads_out = (centered * lax.rsqrt(spread + EPSILON) * gain[...]).astype(BF16)
    partial[...] = dot(heads_out, w_out[...]).astype(BF16)


def ffn_kernel(
    plan, own, by_one, by_two, by_three, p_own, p_one, p_two, p_three, up_first, gain, rates,
    w_up, w_down,
    kept, to_one, to_two, to_three, channel_last,
    entries,
):
    ranks = 4
    feature = own.shape[1]
    tokens = p_own.shape[0]
    count = tokens // 4
    hist_rows = REB * 32
    me = lax.axis_index("head")
    for steps, piece in enumerate((own, by_one, by_two, by_three)):
        block = lax.rem(me - steps + ranks, ranks)
        entries[:, pl.ds(pl.multiple_of(block * feature, feature), feature)] = piece[
            pl.ds(hist_rows, tokens), :
        ].astype(F32)
    mix = sum(piece[...].astype(F32) for piece in (p_own, p_one, p_two, p_three))
    middle = (entries[...] + mix).astype(BF16).astype(F32)
    entries[...] = middle
    own_lanes = pl.ds(pl.multiple_of(me * feature, feature), feature)
    middle_own = entries[:, own_lanes]
    current = normalize(middle, gain[...])
    previous = jnp.concatenate([jnp.zeros_like(current[:count]), current[:-count]], axis=0)
    blended = (current + (previous - current) * rates[4:5, :]).astype(BF16)
    hidden = dot(blended, w_up[...])
    hidden = jnp.concatenate([hidden[:count] + up_first[...], hidden[count:]], axis=0)
    hidden = jnp.maximum(hidden, 0.0)
    hidden = (hidden * hidden).astype(BF16)
    for steps, target in enumerate((kept, to_one, to_two, to_three)):
        block = lax.rem(me + steps, ranks)
        lanes = pl.ds(pl.multiple_of(block * feature, feature), feature)
        rows = dot(hidden, w_down[:, lanes])
        if steps == 0:
            target[...] = rows + middle_own
        else:
            target[...] = rows.astype(BF16)
    occ = column_of(plan, OCCUPIED, count, current.shape[1])
    last = jnp.zeros((count, current.shape[1]), F32)
    for slot in range(4):
        last = jnp.where(occ == slot + 1, current[slot * count : (slot + 1) * count], last)
    entries[pl.ds(0, count), :] = last
    channel_last[...] = entries[pl.ds(0, count), own_lanes]


def on_device(
    arriving_hiddens,
    occupied_slot_totals,
    former_indices,
    reconstruct_marks,
    retained_hiddens,
    carried_memory_matrices,
    lagged_previous_entries,
    pre_attention_scaling,
    pre_feedforward_scaling,
    lag_blend_fractions,
    acceptance_projection,
    address_projection,
    content_projection,
    fading_lowrank_left,
    fading_lowrank_right,
    fading_baseline_entries,
    present_item_reward,
    grouped_layer_scaling,
    attention_exit_projection,
    feedforward_address_proj,
    feedforward_content_proj,
):
    count, steps, feature = arriving_hiddens.shape
    heads = carried_memory_matrices.shape[1]
    channels = heads * WIDTH
    hist = retained_hiddens.shape[1]
    model = pre_attention_scaling.shape[0]
    tokens = count * steps
    row = lambda value: value.reshape(1, -1)
    gathered, packed, plan = call(
        pack_kernel,
        "pack",
        (
            out((REB * hist + tokens + 2 * count, feature), BF16),
            out((count * WIDTH, channels), BF16),
            out((PLAN,), jnp.int32),
        ),
        [
            (former_indices, "scalars"),
            (reconstruct_marks, "scalars"),
            (occupied_slot_totals, "scalars"),
            (retained_hiddens, "any"),
            (carried_memory_matrices, "any"),
            (lagged_previous_entries, "load"),
            (arriving_hiddens, "load"),
        ],
        [
            pltpu.VMEM((tokens + 2 * count, feature), F32),
            pltpu.VMEM((count, heads, WIDTH, WIDTH), F32),
            pltpu.SemaphoreType.DMA((REB,)),
            pltpu.SemaphoreType.DMA((count,)),
        ],
        (VMEM_SPEC, VMEM_SPEC, SMEM_SPEC),
    )
    both = lambda value, stride: (rotate(value, "grp", -stride), rotate(value, "grp", stride))
    plus, minus = both(packed, STRIDES[0])
    pieces = [gathered] + [rotate(gathered, "head", k) for k in (1, 2, 3)]
    base = row(fading_baseline_entries)
    weights = (
        acceptance_projection,
        address_projection,
        content_projection,
        fading_lowrank_left.T,
        feedforward_address_proj,
    )
    inner = fading_lowrank_left.shape[1]
    a_r, a_k, a_v, a_l, rebuilt, aux, hist_first, hist_low, time_last = call(
        project_kernel,
        "project",
        (
            out((tokens, channels), F32),
            out((tokens, channels), F32),
            out((tokens, channels), F32),
            out((tokens, inner), F32),
            out((REB, WIDTH, channels), F32),
            out((AUX * count, channels), BF16),
            out((3, count, channels), F32),
            out((count, inner), F32),
            out((count, feature), F32),
        ),
        [(plan, "smem")]
        + [(value, "vmem") for value in pieces]
        + [(row(pre_attention_scaling), "load"), (lag_blend_fractions, "load")]
        + [(value, "any") for value in weights]
        + [(fading_lowrank_right, "load"), (base, "load")],
        [pltpu.VMEM((REB * hist + tokens + 2 * count, model), F32)]
        + [pltpu.VMEM(value.shape, BF16) for value in weights]
        + [pltpu.SemaphoreType.DMA((len(weights),))],
    )
    aux_plus, aux_minus = both(aux, STRIDES[0])
    moved = call(
        merge_first_kernel,
        "merge0",
        out((count * (WIDTH + AUX), channels), BF16),
        [(plan, "smem")] + [(value, "vmem") for value in (plus, minus, packed, aux_plus, aux_minus, aux)],
    )
    for stage in range(1, len(STRIDES)):
        plus, minus = both(moved, STRIDES[stage])
        moved = call(
            functools.partial(merge_kernel, stage),
            "merge",
            out(moved.shape, BF16),
            [(plan, "smem")] + [(value, "vmem") for value in (plus, minus, moved)],
        )
    next_state, partial, up_first = call(
        recur_kernel,
        "recur",
        (
            out((count, heads, WIDTH, WIDTH), F32),
            out((tokens, model), BF16),
            out((count, feedforward_address_proj.shape[1]), F32),
        ),
        [(plan, "smem")]
        + [(value, "vmem") for value in (moved, hist_first, hist_low, rebuilt, a_r, a_k, a_v, a_l)]
        + [(fading_lowrank_right, "load"), (base, "load")]
        + [(row(present_item_reward), "load"), (row(grouped_layer_scaling), "load")]
        + [(attention_exit_projection, "vmem")],
    )
    partials = [partial] + [rotate(partial, "head", k) for k in (1, 2, 3)]
    kept, to_one, to_two, to_three, channel_last = call(
        ffn_kernel,
        "ffn",
        (
            out((tokens, feature), F32),
            out((tokens, feature), BF16),
            out((tokens, feature), BF16),
            out((tokens, feature), BF16),
            out((count, feature), F32),
        ),
        [(plan, "smem")]
        + [(value, "vmem") for value in (*pieces, *partials, up_first)]
        + [(row(pre_feedforward_scaling), "load"), (lag_blend_fractions, "load")]
        + [(feedforward_address_proj, "vmem"), (feedforward_content_proj, "vmem")],
        [pltpu.VMEM((tokens, model), F32)],
    )
    arrived = [rotate(value, "head", k + 1) for k, value in enumerate((to_one, to_two, to_three))]
    result = kept + sum(value.astype(F32) for value in arrived)
    result = jnp.swapaxes(result.astype(BF16).reshape(steps, count, feature), 0, 1)
    valid_rows = jnp.arange(steps)[None, :] < occupied_slot_totals[:, None]
    result = jnp.where(valid_rows[..., None], result, jnp.zeros_like(result))
    return (result, next_state, jnp.stack([time_last, channel_last], axis=1))


def solution(mesh):
    placed = (
        P("grp", None, "head"),
        P("grp"),
        P("grp"),
        P("grp"),
        P("grp", None, "head"),
        P("grp", "head", None, None),
        P("grp", None, "head"),
        P(),
        P(),
        P(),
        P(None, "head"),
        P(None, "head"),
        P(None, "head"),
        P(),
        P(None, "head"),
        P("head"),
        P("head"),
        P("head"),
        P("head", None),
        P(None, "head"),
        P("head", None),
    )
    return jax.shard_map(
        on_device,
        mesh=mesh,
        in_specs=placed,
        out_specs=(P("grp", None, "head"), P("grp", "head", None, None), P("grp", None, "head")),
        check_vma=False,
    )
```

```python
import functools

import jax
import jax.numpy as jnp
from jax import lax
from jax.experimental import pallas as pl
from jax.experimental.pallas import tpu as pltpu
from jax.sharding import PartitionSpec as P

WIDTH = 64
REB = 2
EPSILON = 1e-05
F32 = jnp.float32
BF16 = jnp.bfloat16
HIGH = lax.Precision.HIGHEST
VMEM_LIMIT = 40 * 1024 * 1024
SMEM_SPEC = pl.BlockSpec(memory_space=pltpu.SMEM)
VMEM_SPEC = pl.BlockSpec(memory_space=pltpu.VMEM)
ANY_SPEC = pl.BlockSpec(memory_space=pl.ANY)


def rotate(value, axis, steps):
    count = lax.axis_size(axis)
    pairs = [(source, (source + steps) % count) for source in range(count)]
    return lax.ppermute(value, axis, pairs)


def on_chip(value):
    return pltpu.with_memory_space_constraint(value, pltpu.VMEM)


def off_chip(value):
    return pltpu.with_memory_space_constraint(value, pltpu.HBM)


SPECS = {"smem": SMEM_SPEC, "vmem": VMEM_SPEC, "load": VMEM_SPEC, "any": ANY_SPEC, "scalars": SMEM_SPEC}
PLACES = {"vmem": on_chip, "load": off_chip, "any": off_chip, "scalars": off_chip}


def call(kernel, name, out_shape, operands, scratch=(), out_specs=None):
    return pl.pallas_call(
        kernel,
        name=name,
        out_shape=out_shape,
        in_specs=[SPECS[place] for _, place in operands],
        out_specs=jax.tree.map(lambda _: VMEM_SPEC, out_shape) if out_specs is None else out_specs,
        scratch_shapes=list(scratch),
        compiler_params=pltpu.CompilerParams(vmem_limit_bytes=VMEM_LIMIT),
    )(*[PLACES.get(place, lambda value: value)(array) for array, place in operands])


def out(shape, dtype):
    return jax.ShapeDtypeStruct(shape, dtype)


def normalize(rows, gain):
    centered = rows - jnp.mean(rows, axis=-1, keepdims=True)
    spread = jnp.mean(centered * centered, axis=-1, keepdims=True)
    return (centered * lax.rsqrt(spread + EPSILON) * gain).astype(BF16).astype(F32)


def dot(left, right, contract=(1, 0), precision=None):
    return lax.dot_general(
        left,
        right,
        (((contract[0],), (contract[1],)), ((), ())),
        precision=precision,
        preferred_element_type=F32,
    )


def halves(value):
    high = value.astype(BF16)
    return high, (value - high.astype(F32)).astype(BF16)


def iota(shape, axis):
    return lax.broadcasted_iota(jnp.int32, shape, axis)


def column_of(plan, base, rows, lanes):
    row = iota((rows, lanes), 0)
    result = jnp.zeros((rows, lanes), jnp.int32)
    for index in range(rows):
        result = jnp.where(row == index, plan[base + index], result)
    return result


def head_blocks(lanes):
    return iota((lanes, lanes), 0) // WIDTH == iota((lanes, lanes), 1) // WIDTH


def head_sums(rows):
    ones = head_blocks(rows.shape[1]).astype(BF16)
    high, low = halves(rows)
    return dot(high, ones) + dot(low, ones)


STRIDES = (24, 3, 8, 1)
SEATS = 5
STAGES = len(STRIDES)
DIGIT, SEAT, PLACE, OCCUPIED, OVER, PLAN = 0, 32, 64, 72, 80, 88
AUX = 7


def signed_residue(value):
    residue = lax.rem(value, 8)
    return jnp.where(residue > 4, residue - 8, residue)


def plan_moves(former, plan, count):
    groups = lax.axis_size("grp")
    here = lax.axis_index("grp")
    distances = [
        lax.rem(lax.div(former[index], count) - here + groups, groups) for index in range(count)
    ]
    one = lambda test: test.astype(jnp.int32)
    over = jnp.int32(0)
    for far, near in ((1, 3), (0, 2)):
        values = [signed_residue(distance) for distance in distances]
        far_up = sum(one((value == 2) | (value == 3)) for value in values)
        far_down = sum(one((value == -2) | (value == -3)) for value in values)
        near_up = sum(one((value == 1) | (value == -2)) for value in values)
        near_down = sum(one((value == -1) | (value == 2)) for value in values)
        up, down = jnp.maximum(far_up, near_up), jnp.maximum(far_down, near_down)
        seats = {(far, 1): 0, (far, -1): 0, (near, 1): 0, (near, -1): 0}
        for index, value in enumerate(values):
            free = value == 4
            rise = free & (up <= down)
            fall = free & (up > down)
            up, down = up + one(rise), down + one(fall)
            value = jnp.where(fall, -4, value)
            distances[index] = lax.div(distances[index] - value + groups, 8)
            triple = one(value >= 2) - one(value <= -2)
            for stage, digit in ((far, triple), (near, value - 3 * triple)):
                plan[DIGIT + stage * count + index] = digit
                seat = jnp.where(digit == 1, seats[stage, 1], seats[stage, -1])
                plan[SEAT + stage * count + index] = jnp.minimum(seat, SEATS - 1)
                for sign in (1, -1):
                    seats[stage, sign] = seats[stage, sign] + one(digit == sign)
        for used in seats.values():
            over = jnp.maximum(over, one(used > SEATS))
    plan[OVER] = over


def seat_rows(plan, stage, index, count):
    seat = plan[SEAT + stage * count + index]
    return pl.ds(pl.multiple_of(seat * WIDTH, WIDTH), WIDTH)


def home_rows(index):
    return pl.ds(index * WIDTH, WIDTH)


def store_row(plan, stage, index, count, value, plus, minus, stay):
    digit = plan[DIGIT + stage * count + index]
    seat = seat_rows(plan, stage, index, count)
    for sign, target, rows in ((1, plus, seat), (-1, minus, seat), (0, stay, home_rows(index))):

        @pl.when(digit == sign)
        def _(target=target, rows=rows):
            target[rows, :] = value()


def load_row(plan, stage, index, count, target, plus, minus, stay):
    digit = plan[DIGIT + stage * count + index]
    seat = seat_rows(plan, stage, index, count)
    for sign, source, rows in ((1, plus, seat), (-1, minus, seat), (0, stay, home_rows(index))):

        @pl.when(digit == sign)
        def _(source=source, rows=rows):
            target[home_rows(index), :] = source[rows, :]


def pack_kernel(
    former, marks, occupied, held, state, shifts, tokens,
    gathered, plus, minus, stay, plan,
    slots, rows, sems, row_sems,
):
    count, heads = rows.shape[0], rows.shape[1]
    hist = held.shape[1]
    sources = [lax.rem(former[index], count) for index in range(count)]
    row_copies = [
        pltpu.make_async_copy(state.at[source], rows.at[index], row_sems.at[index])
        for index, source in enumerate(sources)
    ]
    for copy in row_copies:
        copy.start()
    rank = jnp.int32(0)
    chosen = [jnp.int32(0)] * REB
    for index in range(count):
        marked = marks[index] == 1
        chosen = [
            jnp.where(marked & (rank == place), index, value) for place, value in enumerate(chosen)
        ]
        plan[PLACE + index] = jnp.where(marked, rank, REB)
        rank = rank + marks[index]
        plan[OCCUPIED + index] = occupied[index]
    copies = [
        pltpu.make_async_copy(held.at[value], gathered.at[pl.ds(place * hist, hist)], sems.at[place])
        for place, value in enumerate(chosen)
    ]
    for copy in copies:
        copy.start()
    plan_moves(former, plan, count)
    base = REB * hist
    for index in range(count):
        lines = tokens[index].astype(F32)
        for slot in range(4):
            slots[slot * count + index : slot * count + index + 1, :] = lines[slot : slot + 1]
        line = shifts[sources[index]]
        for which in range(2):
            row = (4 + which) * count + index
            slots[row : row + 1, :] = line[which : which + 1]
    gathered[pl.ds(base, slots.shape[0]), :] = slots[...].astype(BF16)
    for index in range(count):
        row_copies[index].wait()
        whole = rows[index]
        wide = jnp.concatenate([whole[head] for head in range(heads)], axis=1).astype(BF16)
        store_row(plan, 0, index, count, lambda: wide, plus, minus, stay)
    for copy in copies:
        copy.wait()


def pack_all_kernel(former, state, packed, rows, row_sems):
    count, heads = rows.shape[0], rows.shape[1]
    row_copies = [
        pltpu.make_async_copy(state.at[lax.rem(former[index], count)], rows.at[index], row_sems.at[index])
        for index in range(count)
    ]
    for copy in row_copies:
        copy.start()
    for index in range(count):
        row_copies[index].wait()
        whole = rows[index]
        wide = jnp.concatenate([whole[head] for head in range(heads)], axis=1)
        packed[home_rows(index), :] = wide.astype(BF16)


def pick_aux(plan, stage, plus, minus, stay, count):
    shape = (count, plus.shape[1])
    request = iota(shape, 0)
    take = jnp.zeros(shape, jnp.int32)
    for index in range(count):
        take = jnp.where(request == index, plan[DIGIT + stage * count + index], take)
    take = jnp.concatenate([take] * (plus.shape[0] // count), axis=0)
    plus, minus, stay = (value.astype(F32) for value in (plus, minus, stay))
    return jnp.where(take == 1, plus, jnp.where(take == -1, minus, stay)).astype(BF16)


def merge_kernel(stage, count, separate, plan, *refs):
    plus, minus, stay = refs[:3]
    seated, home = SEATS * WIDTH, count * WIDTH
    aux = AUX * count
    if separate:
        aux_values = [ref[...] for ref in refs[3:6]]
        refs = refs[6:]
    else:
        aux_values = [plus[pl.ds(seated, aux), :], minus[pl.ds(seated, aux), :], stay[pl.ds(home, aux), :]]
        refs = refs[3:]
    picked = pick_aux(plan, stage, *aux_values, count)
    if stage + 1 == STAGES:
        (moved,) = refs
        for index in range(count):
            load_row(plan, stage, index, count, moved, plus, minus, stay)
        moved[pl.ds(home, aux), :] = picked
        return
    next_plus, next_minus, next_stay, hold = refs
    for index in range(count):
        load_row(plan, stage, index, count, hold, plus, minus, stay)
    for index in range(count):
        rows = home_rows(index)
        store_row(plan, stage + 1, index, count, lambda: hold[rows, :], next_plus, next_minus, next_stay)
    next_plus[pl.ds(seated, aux), :] = picked
    next_minus[pl.ds(seated, aux), :] = picked
    next_stay[pl.ds(home, aux), :] = picked


def merge_all_kernel(stage, count, plan, plus, minus, stay, moved):
    home, aux = count * WIDTH, AUX * count
    for index in range(count):
        digit = plan[DIGIT + stage * count + index]
        rows = home_rows(index)
        for sign, source in ((1, plus), (-1, minus), (0, stay)):

            @pl.when(digit == sign)
            def _(source=source, rows=rows):
                moved[rows, :] = source[rows, :]

    tail = pl.ds(home, aux)
    moved[tail, :] = pick_aux(plan, stage, plus[tail, :], minus[tail, :], stay[tail, :], count)


def fetch_kernel(*refs):
    count = (len(refs) - 1) // 2
    copies = [
        pltpu.make_async_copy(far, near, refs[-1].at[index])
        for index, (far, near) in enumerate(zip(refs[:count], refs[count:-1]))
    ]
    for copy in copies:
        copy.start()
    for copy in copies:
        copy.wait()


def project_kernel(
    plan, own, by_one, by_two, by_three, gain, rates, w_r, w_k, w_v, w_left, w_up, w_right, base,
    a_r, a_k, a_v, a_l, rebuilt, aux, hist_first, hist_low, time_last,
    entries,
):
    ranks = 4
    feature = own.shape[1]
    hist_rows = REB * 32
    tokens = a_r.shape[0]
    count = tokens // 4
    normal = hist_rows + tokens
    me = lax.axis_index("head")
    for steps, piece in enumerate((own, by_one, by_two, by_three)):
        block = lax.rem(me - steps + ranks, ranks)
        entries[:, pl.ds(pl.multiple_of(block * feature, feature), feature)] = piece[...].astype(F32)
    current = normalize(entries[pl.ds(0, normal), :], gain[...])
    hist = current[:hist_rows]
    live = current[hist_rows:]
    place = iota(hist.shape, 0) % 32
    hist_previous = jnp.where(place == 0, 0.0, pltpu.roll(hist, 1, 0))
    live_previous = jnp.concatenate([jnp.zeros_like(live[:count]), live[:-count]], axis=0)
    previous = jnp.concatenate([hist_previous, live_previous], axis=0)
    change = previous - current
    moved_shift = entries[pl.ds(normal, count), :]
    lines = iota(moved_shift.shape, 0)
    last_hist = jnp.zeros_like(moved_shift)
    for slot in range(REB):
        last_hist = jnp.where(lines == slot, hist[slot * 32 + 31 : slot * 32 + 32], last_hist)
    first = jnp.concatenate([moved_shift, last_hist], axis=0)

    def mixed(which):
        rate = rates[which : which + 1, :]
        return jnp.concatenate([current + change * rate, first * rate], axis=0).astype(BF16)

    keys = dot(mixed(1), w_k[...])
    values = dot(mixed(2), w_v[...])
    low = dot(mixed(3), w_left[...], (1, 1))
    received = dot(mixed(0)[hist_rows:], w_r[...])
    a_r[...] = received[:tokens]
    a_k[...] = keys[hist_rows:normal]
    a_v[...] = values[hist_rows:normal]
    a_l[...] = low[hist_rows:normal]
    hist_first[0] = received[tokens + count :]
    hist_first[1] = keys[normal + count :]
    hist_first[2] = values[normal + count :]
    hist_low[...] = low[normal + count :]
    up = dot((entries[pl.ds(normal + count, count), :] * rates[4:5, :]).astype(BF16), w_up[...])
    lanes = aux.shape[1]
    whole = up.shape[1] // lanes
    left = jnp.concatenate([low[normal : normal + count], jnp.zeros((count, lanes // 2 - low.shape[1]), F32)], axis=1)
    moving = [received[tokens : tokens + count], keys[normal : normal + count], values[normal : normal + count]]
    moving += [up[:, part * lanes : (part + 1) * lanes] for part in range(whole)]
    moving += [jnp.concatenate([left, up[:, whole * lanes :]], axis=1)]
    aux[...] = jnp.concatenate(moving, axis=0).astype(BF16)
    keys, values, low = keys[:hist_rows], values[:hist_rows], low[:hist_rows]
    rank = jnp.tanh(low).astype(BF16)
    decay = jnp.exp(-jnp.exp(base[...] + dot(rank, w_right[...])))
    spot = iota(decay.shape, 0) % 32
    product = decay
    for steps in (1, 2, 4, 8, 16):
        product = product * jnp.where(spot + steps < 32, pltpu.roll(product, hist_rows - steps, 0), 1.0)
    later = jnp.where(spot < 31, pltpu.roll(product, hist_rows - 1, 0), 1.0)
    keys = keys * later
    lane = iota((WIDTH, values.shape[1]), 1) // WIDTH
    for slot in range(REB):
        span = slice(slot * 32, slot * 32 + 32)
        k_high, k_low = halves(keys[span])
        v_high, v_low = halves(values[span])
        outer = dot(
            jnp.concatenate([k_high, k_high, k_low], axis=0),
            jnp.concatenate([v_high, v_low, v_high], axis=0),
            (0, 0),
        )
        packed = outer[:WIDTH]
        for which in range(1, values.shape[1] // WIDTH):
            packed = jnp.where(lane == which, outer[which * WIDTH : (which + 1) * WIDTH], packed)
        rebuilt[slot] = packed
    occ = column_of(plan, OCCUPIED, count, current.shape[1])
    last = jnp.zeros((count, current.shape[1]), F32)
    for slot in range(4):
        last = jnp.where(occ == slot + 1, live[slot * count : (slot + 1) * count], last)
    entries[pl.ds(0, count), :] = last
    time_last[...] = entries[pl.ds(0, count), pl.ds(pl.multiple_of(me * feature, feature), feature)]


def recur_kernel(
    plan, moved, hist_first, hist_low, rebuilt, a_r, a_k, a_v, a_l, w_right, base, reward, gain, w_out,
    next_state, partial, up_first,
):
    count = next_state.shape[0]
    channels = a_r.shape[1]
    place = [plan[PLACE + index] for index in range(count)]
    slots = column_of(plan, PLACE, count, channels)
    aux = moved[pl.ds(count * WIDTH, AUX * count), :].astype(F32)
    block = lambda part: aux[part * count : (part + 1) * count]
    inner = hist_low.shape[1]

    def with_first(rows, extra, hist):
        for slot in range(REB):
            extra = jnp.where(slots[:, : extra.shape[1]] == slot, hist[slot : slot + 1, :], extra)
        return jnp.concatenate([rows[:count] + extra, rows[count:]], axis=0)

    received = with_first(a_r[...], block(0), hist_first[0])
    keys = with_first(a_k[...], block(1), hist_first[1])
    values = with_first(a_v[...], block(2), hist_first[2])
    low = jnp.tanh(with_first(a_l[...], block(6)[:, :inner], hist_low[...])).astype(BF16)
    up_first[...] = jnp.concatenate([block(3), block(4), block(5), block(6)[:, channels // 2 :]], axis=1)
    decay = jnp.exp(-jnp.exp(base[...] + dot(low, w_right[...])))
    occ = column_of(plan, OCCUPIED, count, channels)
    slot_of = lambda rows: [rows[slot * count : (slot + 1) * count] for slot in range(4)]
    r, k, v, d = slot_of(received), slot_of(keys), slot_of(values), slot_of(decay)
    d = [jnp.where(occ > slot, d[slot], 1.0) for slot in range(4)]
    k_live = [jnp.where(occ > slot, k[slot], 0.0) for slot in range(4)]
    before = [jnp.ones_like(d[0])]
    for slot in range(4):
        before.append(before[-1] * d[slot])
    query = jnp.concatenate([r[slot] * before[slot] for slot in range(4)], axis=0)
    scores, pairs = [], []
    for slot in range(4):
        scores.append(r[slot] * reward[...] * k[slot])
        pairs.append((slot, slot))
        between = jnp.ones_like(d[0])
        for earlier in range(slot - 1, -1, -1):
            scores.append(r[slot] * between * k_live[earlier])
            pairs.append((slot, earlier))
            between = between * d[earlier]
    sums = head_sums(jnp.concatenate(scores, axis=0))
    inner = [jnp.zeros_like(v[0])] * 4
    for index, (slot, earlier) in enumerate(pairs):
        inner[slot] = inner[slot] + sums[index * count : (index + 1) * count] * v[earlier]
    mixed = jnp.concatenate(inner, axis=0)
    after = jnp.ones_like(d[0])
    k_after = [None] * 4
    for slot in range(3, -1, -1):
        k_after[slot] = k_live[slot] * after
        after = after * d[slot]
    k_high, k_low = halves(jnp.concatenate(k_after, axis=0))
    v_high, v_low = halves(values)
    k_rows = jnp.concatenate([k_high, k_high, k_low], axis=0)
    v_rows = jnp.concatenate([v_high, v_low, v_high], axis=0).astype(F32)
    k_columns = jnp.transpose(k_rows.astype(F32)).astype(BF16)
    after_columns = jnp.transpose(before[4])
    q_high, q_low = halves(query)
    q_rows = jnp.concatenate([q_high, q_low], axis=0).astype(F32)
    q_request = iota(q_rows.shape, 0) % count
    v_request = iota(v_rows.shape, 0) % count
    blocks = head_blocks(channels)
    total = jnp.zeros((q_rows.shape[0], channels), F32)
    for index in range(count):
        packed = moved[pl.ds(index * WIDTH, WIDTH), :].astype(F32)
        for slot in range(REB):
            packed = jnp.where(place[index] == slot, rebuilt[slot], packed)
        tall = jnp.concatenate([packed] * (channels // WIDTH), axis=0)
        tall = jnp.where(blocks, tall, 0.0).astype(BF16)
        total = total + dot(jnp.where(q_request == index, q_rows, 0.0).astype(BF16), tall)
        update = dot(k_columns, jnp.where(v_request == index, v_rows, 0.0).astype(BF16))
        for which in range(channels // WIDTH):
            rows = slice(which * WIDTH, (which + 1) * WIDTH)
            lanes = slice(which // 2 * 128, which // 2 * 128 + 128)
            block = update[rows, lanes] + after_columns[rows, index : index + 1] * packed[:, lanes]
            if which % 2:
                block = pltpu.roll(block, 64, 1)
            next_state[index, which] = block[:, :WIDTH]
    mixed = mixed + total[: 4 * count] + total[4 * count :]
    centered = mixed - head_sums(mixed) * (1.0 / WIDTH)
    spread = head_sums(centered * centered) * (1.0 / WIDTH)
    heads_out = (centered * lax.rsqrt(spread + EPSILON) * gain[...]).astype(BF16)
    partial[...] = dot(heads_out, w_out[...]).astype(BF16)


def ffn_kernel(
    plan, own, by_one, by_two, by_three, p_own, p_one, p_two, p_three, up_first, gain, rates,
    w_up, w_down,
    kept, to_one, to_two, to_three, channel_last,
    entries,
):
    ranks = 4
    feature = own.shape[1]
    tokens = p_own.shape[0]
    count = tokens // 4
    hist_rows = REB * 32
    me = lax.axis_index("head")
    for steps, piece in enumerate((own, by_one, by_two, by_three)):
        block = lax.rem(me - steps + ranks, ranks)
        entries[:, pl.ds(pl.multiple_of(block * feature, feature), feature)] = piece[
            pl.ds(hist_rows, tokens), :
        ].astype(F32)
    mix = sum(piece[...].astype(F32) for piece in (p_own, p_one, p_two, p_three))
    middle = (entries[...] + mix).astype(BF16).astype(F32)
    entries[...] = middle
    own_lanes = pl.ds(pl.multiple_of(me * feature, feature), feature)
    middle_own = entries[:, own_lanes]
    current = normalize(middle, gain[...])
    previous = jnp.concatenate([jnp.zeros_like(current[:count]), current[:-count]], axis=0)
    blended = (current + (previous - current) * rates[4:5, :]).astype(BF16)
    hidden = dot(blended, w_up[...])
    hidden = jnp.concatenate([hidden[:count] + up_first[...], hidden[count:]], axis=0)
    hidden = jnp.maximum(hidden, 0.0)
    hidden = (hidden * hidden).astype(BF16)
    for steps, target in enumerate((kept, to_one, to_two, to_three)):
        block = lax.rem(me + steps, ranks)
        lanes = pl.ds(pl.multiple_of(block * feature, feature), feature)
        rows = dot(hidden, w_down[:, lanes])
        if steps == 0:
            target[...] = rows + middle_own
        else:
            target[...] = rows.astype(BF16)
    occ = column_of(plan, OCCUPIED, count, current.shape[1])
    last = jnp.zeros((count, current.shape[1]), F32)
    for slot in range(4):
        last = jnp.where(occ == slot + 1, current[slot * count : (slot + 1) * count], last)
    entries[pl.ds(0, count), :] = last
    channel_last[...] = entries[pl.ds(0, count), own_lanes]


def on_device(
    arriving_hiddens,
    occupied_slot_totals,
    former_indices,
    reconstruct_marks,
    retained_hiddens,
    carried_memory_matrices,
    lagged_previous_entries,
    pre_attention_scaling,
    pre_feedforward_scaling,
    lag_blend_fractions,
    acceptance_projection,
    address_projection,
    content_projection,
    fading_lowrank_left,
    fading_lowrank_right,
    fading_baseline_entries,
    present_item_reward,
    grouped_layer_scaling,
    attention_exit_projection,
    feedforward_address_proj,
    feedforward_content_proj,
):
    count, steps, feature = arriving_hiddens.shape
    heads = carried_memory_matrices.shape[1]
    channels = heads * WIDTH
    hist = retained_hiddens.shape[1]
    model = pre_attention_scaling.shape[0]
    tokens = count * steps
    row = lambda value: value.reshape(1, -1)
    home, seated, aux_rows = count * WIDTH, SEATS * WIDTH, AUX * count
    gathered, plus, minus, stay, plan = call(
        pack_kernel,
        "pack",
        (
            out((REB * hist + tokens + 2 * count, feature), BF16),
            out((seated, channels), BF16),
            out((seated, channels), BF16),
            out((home, channels), BF16),
            out((PLAN,), jnp.int32),
        ),
        [
            (former_indices, "scalars"),
            (reconstruct_marks, "scalars"),
            (occupied_slot_totals, "scalars"),
            (retained_hiddens, "any"),
            (carried_memory_matrices, "any"),
            (lagged_previous_entries, "load"),
            (arriving_hiddens, "load"),
        ],
        [
            pltpu.VMEM((tokens + 2 * count, feature), F32),
            pltpu.VMEM((count, heads, WIDTH, WIDTH), F32),
            pltpu.SemaphoreType.DMA((REB,)),
            pltpu.SemaphoreType.DMA((count,)),
        ],
        (VMEM_SPEC, VMEM_SPEC, VMEM_SPEC, VMEM_SPEC, SMEM_SPEC),
    )

    def send(stage, up, down):
        return rotate(up, "grp", -STRIDES[stage]), rotate(down, "grp", STRIDES[stage])

    plus, minus = send(0, plus, minus)
    pieces = [gathered] + [rotate(gathered, "head", k) for k in (1, 2, 3)]
    base = row(fading_baseline_entries)
    far_weights = (
        acceptance_projection,
        address_projection,
        content_projection,
        fading_lowrank_left.T,
        feedforward_address_proj,
    )

    def fetch(values, after):
        values, _ = lax.optimization_barrier((values, after))
        return call(
            fetch_kernel,
            "fetch",
            tuple(out(value.shape, BF16) for value in values),
            [(value, "any") for value in values],
            [pltpu.SemaphoreType.DMA((len(values),))],
        )

    weights = fetch(far_weights, gathered)
    inner = fading_lowrank_left.shape[1]
    a_r, a_k, a_v, a_l, rebuilt, aux, hist_first, hist_low, time_last = call(
        project_kernel,
        "project",
        (
            out((tokens, channels), F32),
            out((tokens, channels), F32),
            out((tokens, channels), F32),
            out((tokens, inner), F32),
            out((REB, WIDTH, channels), F32),
            out((AUX * count, channels), BF16),
            out((3, count, channels), F32),
            out((count, inner), F32),
            out((count, feature), F32),
        ),
        [(plan, "smem")]
        + [(value, "vmem") for value in pieces]
        + [(row(pre_attention_scaling), "load"), (lag_blend_fractions, "load")]
        + [(value, "vmem") for value in weights]
        + [(fading_lowrank_right, "load"), (base, "load")],
        [pltpu.VMEM((REB * hist + tokens + 2 * count, model), F32)],
    )
    arrived = (plus, minus, stay, *send(0, aux, aux), aux)
    shape = lambda rows: out((rows + aux_rows, channels), BF16)
    for stage in range(STAGES):
        last = stage + 1 == STAGES
        merged = call(
            functools.partial(merge_kernel, stage, count, stage == 0),
            "merge",
            shape(home) if last else (shape(seated), shape(seated), shape(home)),
            [(plan, "smem")] + [(value, "vmem") for value in arrived],
            [] if last else [pltpu.VMEM((home, channels), BF16)],
        )
        if not last:
            arrived = (*send(stage + 1, *merged[:2]), merged[2])

    def move_all(moved, aux, plan, former, state):
        packed = call(
            pack_all_kernel,
            "pack_all",
            out((home, channels), BF16),
            [(former, "scalars"), (state, "any")],
            [pltpu.VMEM((count, heads, WIDTH, WIDTH), F32), pltpu.SemaphoreType.DMA((count,))],
        )
        moved = jnp.concatenate([packed, aux], axis=0)
        for stage in range(STAGES):
            moved = call(
                functools.partial(merge_all_kernel, stage, count),
                "merge_all",
                shape(home),
                [(plan, "smem")] + [(value, "load") for value in (*send(stage, moved, moved), moved)],
            )
        return moved

    moved = lax.cond(
        plan[OVER] > 0,
        move_all,
        lambda moved, *_: moved,
        merged,
        aux,
        plan,
        former_indices,
        carried_memory_matrices,
    )
    next_state, partial, up_first = call(
        recur_kernel,
        "recur",
        (
            out((count, heads, WIDTH, WIDTH), F32),
            out((tokens, model), BF16),
            out((count, feedforward_address_proj.shape[1]), F32),
        ),
        [(plan, "smem")]
        + [(value, "vmem") for value in (moved, hist_first, hist_low, rebuilt, a_r, a_k, a_v, a_l)]
        + [(fading_lowrank_right, "load"), (base, "load")]
        + [(row(present_item_reward), "load"), (row(grouped_layer_scaling), "load")]
        + [(attention_exit_projection, "vmem")],
    )
    partials = [partial] + [rotate(partial, "head", k) for k in (1, 2, 3)]
    ffn_weights = fetch((feedforward_address_proj, feedforward_content_proj), partial)
    kept, to_one, to_two, to_three, channel_last = call(
        ffn_kernel,
        "ffn",
        (
            out((tokens, feature), F32),
            out((tokens, feature), BF16),
            out((tokens, feature), BF16),
            out((tokens, feature), BF16),
            out((count, feature), F32),
        ),
        [(plan, "smem")]
        + [(value, "vmem") for value in (*pieces, *partials, up_first)]
        + [(row(pre_feedforward_scaling), "load"), (lag_blend_fractions, "load")]
        + [(value, "vmem") for value in ffn_weights],
        [pltpu.VMEM((tokens, model), F32)],
    )
    arrived = [rotate(value, "head", k + 1) for k, value in enumerate((to_one, to_two, to_three))]
    result = kept + sum(value.astype(F32) for value in arrived)
    result = jnp.swapaxes(result.astype(BF16).reshape(steps, count, feature), 0, 1)
    valid_rows = jnp.arange(steps)[None, :] < occupied_slot_totals[:, None]
    result = jnp.where(valid_rows[..., None], result, jnp.zeros_like(result))
    return (result, next_state, jnp.stack([time_last, channel_last], axis=1))


def solution(mesh):
    placed = (
        P("grp", None, "head"),
        P("grp"),
        P("grp"),
        P("grp"),
        P("grp", None, "head"),
        P("grp", "head", None, None),
        P("grp", None, "head"),
        P(),
        P(),
        P(),
        P(None, "head"),
        P(None, "head"),
        P(None, "head"),
        P(),
        P(None, "head"),
        P("head"),
        P("head"),
        P("head"),
        P("head", None),
        P(None, "head"),
        P("head", None),
    )
    return jax.shard_map(
        on_device,
        mesh=mesh,
        in_specs=placed,
        out_specs=(P("grp", None, "head"), P("grp", "head", None, None), P("grp", None, "head")),
        check_vma=False,
    )
```

```python
import functools

import jax
import jax.numpy as jnp
from jax import lax
from jax.experimental import pallas as pl
from jax.experimental.pallas import tpu as pltpu
from jax.sharding import PartitionSpec as P

WIDTH = 64
REB = 2
EPSILON = 1e-05
F32 = jnp.float32
BF16 = jnp.bfloat16
HIGH = lax.Precision.HIGHEST
VMEM_LIMIT = 40 * 1024 * 1024
SMEM_SPEC = pl.BlockSpec(memory_space=pltpu.SMEM)
VMEM_SPEC = pl.BlockSpec(memory_space=pltpu.VMEM)
ANY_SPEC = pl.BlockSpec(memory_space=pl.ANY)


def rotate(value, axis, steps):
    count = lax.axis_size(axis)
    pairs = [(source, (source + steps) % count) for source in range(count)]
    return lax.ppermute(value, axis, pairs)


def on_chip(value):
    return pltpu.with_memory_space_constraint(value, pltpu.VMEM)


def off_chip(value):
    return pltpu.with_memory_space_constraint(value, pltpu.HBM)


SPECS = {"smem": SMEM_SPEC, "vmem": VMEM_SPEC, "load": VMEM_SPEC, "any": ANY_SPEC, "scalars": SMEM_SPEC}
PLACES = {"vmem": on_chip, "load": off_chip, "any": off_chip, "scalars": off_chip}


def call(kernel, name, out_shape, operands, scratch=(), out_specs=None, cost=None):
    return pl.pallas_call(
        kernel,
        name=name,
        out_shape=out_shape,
        in_specs=[SPECS[place] for _, place in operands],
        out_specs=jax.tree.map(lambda _: VMEM_SPEC, out_shape) if out_specs is None else out_specs,
        scratch_shapes=list(scratch),
        cost_estimate=cost,
        compiler_params=pltpu.CompilerParams(vmem_limit_bytes=VMEM_LIMIT),
    )(*[PLACES.get(place, lambda value: value)(array) for array, place in operands])


def out(shape, dtype):
    return jax.ShapeDtypeStruct(shape, dtype)


def normalize(rows, gain):
    centered = rows - jnp.mean(rows, axis=-1, keepdims=True)
    spread = jnp.mean(centered * centered, axis=-1, keepdims=True)
    return (centered * lax.rsqrt(spread + EPSILON) * gain).astype(BF16).astype(F32)


def dot(left, right, contract=(1, 0), precision=None):
    return lax.dot_general(
        left,
        right,
        (((contract[0],), (contract[1],)), ((), ())),
        precision=precision,
        preferred_element_type=F32,
    )


def halves(value):
    high = value.astype(BF16)
    return high, (value - high.astype(F32)).astype(BF16)


def iota(shape, axis):
    return lax.broadcasted_iota(jnp.int32, shape, axis)


def column_of(plan, base, rows, lanes):
    row = iota((rows, lanes), 0)
    result = jnp.zeros((rows, lanes), jnp.int32)
    for index in range(rows):
        result = jnp.where(row == index, plan[base + index], result)
    return result


def head_blocks(lanes):
    return iota((lanes, lanes), 0) // WIDTH == iota((lanes, lanes), 1) // WIDTH


def head_sums(rows):
    ones = head_blocks(rows.shape[1]).astype(BF16)
    high, low = halves(rows)
    return dot(high, ones) + dot(low, ones)


STRIDES = (24, 3, 8, 1)
SEATS = 5
STAGES = len(STRIDES)
DIGIT, SEAT, PLACE, OCCUPIED, OVER, PLAN = 0, 32, 64, 72, 80, 88
AUX = 7


def signed_residue(value):
    residue = lax.rem(value, 8)
    return jnp.where(residue > 4, residue - 8, residue)


def plan_moves(former, plan, count):
    groups = lax.axis_size("grp")
    here = lax.axis_index("grp")
    distances = [
        lax.rem(lax.div(former[index], count) - here + groups, groups) for index in range(count)
    ]
    one = lambda test: test.astype(jnp.int32)
    over = jnp.int32(0)
    for far, near in ((1, 3), (0, 2)):
        values = [signed_residue(distance) for distance in distances]
        far_up = sum(one((value == 2) | (value == 3)) for value in values)
        far_down = sum(one((value == -2) | (value == -3)) for value in values)
        near_up = sum(one((value == 1) | (value == -2)) for value in values)
        near_down = sum(one((value == -1) | (value == 2)) for value in values)
        up, down = jnp.maximum(far_up, near_up), jnp.maximum(far_down, near_down)
        seats = {(far, 1): 0, (far, -1): 0, (near, 1): 0, (near, -1): 0}
        for index, value in enumerate(values):
            free = value == 4
            rise = free & (up <= down)
            fall = free & (up > down)
            up, down = up + one(rise), down + one(fall)
            value = jnp.where(fall, -4, value)
            distances[index] = lax.div(distances[index] - value + groups, 8)
            triple = one(value >= 2) - one(value <= -2)
            for stage, digit in ((far, triple), (near, value - 3 * triple)):
                plan[DIGIT + stage * count + index] = digit
                seat = jnp.where(digit == 1, seats[stage, 1], seats[stage, -1])
                plan[SEAT + stage * count + index] = jnp.minimum(seat, SEATS - 1)
                for sign in (1, -1):
                    seats[stage, sign] = seats[stage, sign] + one(digit == sign)
        for used in seats.values():
            over = jnp.maximum(over, one(used > SEATS))
    plan[OVER] = over


def seat_rows(plan, stage, index, count):
    seat = plan[SEAT + stage * count + index]
    return pl.ds(pl.multiple_of(seat * WIDTH, WIDTH), WIDTH)


def home_rows(index):
    return pl.ds(index * WIDTH, WIDTH)


def store_row(plan, stage, index, count, value, plus, minus, stay):
    digit = plan[DIGIT + stage * count + index]
    seat = seat_rows(plan, stage, index, count)
    for sign, target, rows in ((1, plus, seat), (-1, minus, seat), (0, stay, home_rows(index))):

        @pl.when(digit == sign)
        def _(target=target, rows=rows):
            target[rows, :] = value()


def load_row(plan, stage, index, count, target, plus, minus, stay):
    digit = plan[DIGIT + stage * count + index]
    seat = seat_rows(plan, stage, index, count)
    for sign, source, rows in ((1, plus, seat), (-1, minus, seat), (0, stay, home_rows(index))):

        @pl.when(digit == sign)
        def _(source=source, rows=rows):
            target[home_rows(index), :] = source[rows, :]


def pack_kernel(
    former, marks, occupied, held, state, shifts, tokens, far_r, far_k, far_v, far_left,
    gathered, plus, minus, stay, w_r, w_k, w_v, w_left, plan,
    slots, rows, sems, row_sems, weight_sems,
):
    count, heads = rows.shape[0], rows.shape[1]
    hist = held.shape[1]
    sources = [lax.rem(former[index], count) for index in range(count)]
    row_copies = [
        pltpu.make_async_copy(state.at[source], rows.at[index], row_sems.at[index])
        for index, source in enumerate(sources)
    ]
    for copy in row_copies:
        copy.start()
    far = (far_r, far_k, far_v, far_left)
    weight_copies = [
        pltpu.make_async_copy(source, target, weight_sems.at[index])
        for index, (source, target) in enumerate(zip(far, (w_r, w_k, w_v, w_left)))
    ]
    for copy in weight_copies:
        copy.start()
    rank = jnp.int32(0)
    chosen = [jnp.int32(0)] * REB
    for index in range(count):
        marked = marks[index] == 1
        chosen = [
            jnp.where(marked & (rank == place), index, value) for place, value in enumerate(chosen)
        ]
        plan[PLACE + index] = jnp.where(marked, rank, REB)
        rank = rank + marks[index]
        plan[OCCUPIED + index] = occupied[index]
    copies = [
        pltpu.make_async_copy(held.at[value], gathered.at[pl.ds(place * hist, hist)], sems.at[place])
        for place, value in enumerate(chosen)
    ]
    for copy in copies:
        copy.start()
    plan_moves(former, plan, count)
    base = REB * hist
    for index in range(count):
        lines = tokens[index].astype(F32)
        for slot in range(4):
            slots[slot * count + index : slot * count + index + 1, :] = lines[slot : slot + 1]
        line = shifts[sources[index]]
        for which in range(2):
            row = (4 + which) * count + index
            slots[row : row + 1, :] = line[which : which + 1]
    gathered[pl.ds(base, slots.shape[0]), :] = slots[...].astype(BF16)
    for index in range(count):
        row_copies[index].wait()
        whole = rows[index]
        wide = jnp.concatenate([whole[head] for head in range(heads)], axis=1).astype(BF16)
        store_row(plan, 0, index, count, lambda: wide, plus, minus, stay)
    for copy in copies + weight_copies:
        copy.wait()


def pack_all_kernel(former, state, packed, rows, row_sems):
    count, heads = rows.shape[0], rows.shape[1]
    row_copies = [
        pltpu.make_async_copy(state.at[lax.rem(former[index], count)], rows.at[index], row_sems.at[index])
        for index in range(count)
    ]
    for copy in row_copies:
        copy.start()
    for index in range(count):
        row_copies[index].wait()
        whole = rows[index]
        wide = jnp.concatenate([whole[head] for head in range(heads)], axis=1)
        packed[home_rows(index), :] = wide.astype(BF16)


def pick_aux(plan, stage, plus, minus, stay, count):
    shape = (count, plus.shape[1])
    request = iota(shape, 0)
    take = jnp.zeros(shape, jnp.int32)
    for index in range(count):
        take = jnp.where(request == index, plan[DIGIT + stage * count + index], take)
    take = jnp.concatenate([take] * (plus.shape[0] // count), axis=0)
    plus, minus, stay = (value.astype(F32) for value in (plus, minus, stay))
    return jnp.where(take == 1, plus, jnp.where(take == -1, minus, stay)).astype(BF16)


def merge_kernel(stage, count, separate, plan, *refs):
    plus, minus, stay = refs[:3]
    seated, home = SEATS * WIDTH, count * WIDTH
    aux = AUX * count
    if separate:
        aux_values = [ref[...] for ref in refs[3:6]]
        refs = refs[6:]
    else:
        aux_values = [plus[pl.ds(seated, aux), :], minus[pl.ds(seated, aux), :], stay[pl.ds(home, aux), :]]
        refs = refs[3:]
    picked = pick_aux(plan, stage, *aux_values, count)
    if stage + 1 == STAGES:
        (moved,) = refs
        for index in range(count):
            load_row(plan, stage, index, count, moved, plus, minus, stay)
        moved[pl.ds(home, aux), :] = picked
        return
    next_plus, next_minus, next_stay, hold = refs
    for index in range(count):
        load_row(plan, stage, index, count, hold, plus, minus, stay)
    for index in range(count):
        rows = home_rows(index)
        store_row(plan, stage + 1, index, count, lambda: hold[rows, :], next_plus, next_minus, next_stay)
    next_plus[pl.ds(seated, aux), :] = picked
    next_minus[pl.ds(seated, aux), :] = picked
    next_stay[pl.ds(home, aux), :] = picked


def merge_all_kernel(stage, count, plan, plus, minus, stay, moved):
    home, aux = count * WIDTH, AUX * count
    for index in range(count):
        digit = plan[DIGIT + stage * count + index]
        rows = home_rows(index)
        for sign, source in ((1, plus), (-1, minus), (0, stay)):

            @pl.when(digit == sign)
            def _(source=source, rows=rows):
                moved[rows, :] = source[rows, :]

    tail = pl.ds(home, aux)
    moved[tail, :] = pick_aux(plan, stage, plus[tail, :], minus[tail, :], stay[tail, :], count)


def fetch_kernel(*refs):
    count = (len(refs) - 1) // 2
    copies = [
        pltpu.make_async_copy(far, near, refs[-1].at[index])
        for index, (far, near) in enumerate(zip(refs[:count], refs[count:-1]))
    ]
    for copy in copies:
        copy.start()
    for copy in copies:
        copy.wait()


def project_kernel(
    plan, own, by_one, by_two, by_three, gain, rates, w_r, w_k, w_v, w_left, far_up, w_right, base,
    a_r, a_k, a_v, a_l, rebuilt, aux, hist_first, hist_low, time_last,
    entries, w_up, up_sem,
):
    fetch_up = pltpu.make_async_copy(far_up, w_up, up_sem.at[0])
    fetch_up.start()
    ranks = 4
    feature = own.shape[1]
    hist_rows = REB * 32
    tokens = a_r.shape[0]
    count = tokens // 4
    normal = hist_rows + tokens
    me = lax.axis_index("head")
    for steps, piece in enumerate((own, by_one, by_two, by_three)):
        block = lax.rem(me - steps + ranks, ranks)
        entries[:, pl.ds(pl.multiple_of(block * feature, feature), feature)] = piece[...].astype(F32)
    current = normalize(entries[pl.ds(0, normal), :], gain[...])
    hist = current[:hist_rows]
    live = current[hist_rows:]
    place = iota(hist.shape, 0) % 32
    hist_previous = jnp.where(place == 0, 0.0, pltpu.roll(hist, 1, 0))
    live_previous = jnp.concatenate([jnp.zeros_like(live[:count]), live[:-count]], axis=0)
    previous = jnp.concatenate([hist_previous, live_previous], axis=0)
    change = previous - current
    moved_shift = entries[pl.ds(normal, count), :]
    lines = iota(moved_shift.shape, 0)
    last_hist = jnp.zeros_like(moved_shift)
    for slot in range(REB):
        last_hist = jnp.where(lines == slot, hist[slot * 32 + 31 : slot * 32 + 32], last_hist)
    first = jnp.concatenate([moved_shift, last_hist], axis=0)

    def mixed(which):
        rate = rates[which : which + 1, :]
        return jnp.concatenate([current + change * rate, first * rate], axis=0).astype(BF16)

    keys = dot(mixed(1), w_k[...])
    values = dot(mixed(2), w_v[...])
    low = dot(mixed(3), w_left[...], (1, 1))
    received = dot(mixed(0)[hist_rows:], w_r[...])
    a_r[...] = received[:tokens]
    a_k[...] = keys[hist_rows:normal]
    a_v[...] = values[hist_rows:normal]
    a_l[...] = low[hist_rows:normal]
    hist_first[0] = received[tokens + count :]
    hist_first[1] = keys[normal + count :]
    hist_first[2] = values[normal + count :]
    hist_low[...] = low[normal + count :]
    moving = [received[tokens : tokens + count], keys[normal : normal + count], values[normal : normal + count]]
    low_moving = low[normal : normal + count]
    keys, values, low = keys[:hist_rows], values[:hist_rows], low[:hist_rows]
    rank = jnp.tanh(low).astype(BF16)
    decay = jnp.exp(-jnp.exp(base[...] + dot(rank, w_right[...])))
    spot = iota(decay.shape, 0) % 32
    product = decay
    for steps in (1, 2, 4, 8, 16):
        product = product * jnp.where(spot + steps < 32, pltpu.roll(product, hist_rows - steps, 0), 1.0)
    later = jnp.where(spot < 31, pltpu.roll(product, hist_rows - 1, 0), 1.0)
    keys = keys * later
    lane = iota((WIDTH, values.shape[1]), 1) // WIDTH
    for slot in range(REB):
        span = slice(slot * 32, slot * 32 + 32)
        k_high, k_low = halves(keys[span])
        v_high, v_low = halves(values[span])
        outer = dot(
            jnp.concatenate([k_high, k_high, k_low], axis=0),
            jnp.concatenate([v_high, v_low, v_high], axis=0),
            (0, 0),
        )
        packed = outer[:WIDTH]
        for which in range(1, values.shape[1] // WIDTH):
            packed = jnp.where(lane == which, outer[which * WIDTH : (which + 1) * WIDTH], packed)
        rebuilt[slot] = packed
    fetch_up.wait()
    up = dot((entries[pl.ds(normal + count, count), :] * rates[4:5, :]).astype(BF16), w_up[...])
    lanes = aux.shape[1]
    whole = up.shape[1] // lanes
    left = jnp.concatenate([low_moving, jnp.zeros((count, lanes // 2 - low_moving.shape[1]), F32)], axis=1)
    moving += [up[:, part * lanes : (part + 1) * lanes] for part in range(whole)]
    moving += [jnp.concatenate([left, up[:, whole * lanes :]], axis=1)]
    aux[...] = jnp.concatenate(moving, axis=0).astype(BF16)
    occ = column_of(plan, OCCUPIED, count, current.shape[1])
    last = jnp.zeros((count, current.shape[1]), F32)
    for slot in range(4):
        last = jnp.where(occ == slot + 1, live[slot * count : (slot + 1) * count], last)
    entries[pl.ds(0, count), :] = last
    time_last[...] = entries[pl.ds(0, count), pl.ds(pl.multiple_of(me * feature, feature), feature)]


def recur_kernel(
    plan, moved, hist_first, hist_low, rebuilt, a_r, a_k, a_v, a_l, w_right, base, reward, gain, w_out,
    next_state, partial, up_first,
):
    count = next_state.shape[0]
    channels = a_r.shape[1]
    place = [plan[PLACE + index] for index in range(count)]
    slots = column_of(plan, PLACE, count, channels)
    aux = moved[pl.ds(count * WIDTH, AUX * count), :].astype(F32)
    block = lambda part: aux[part * count : (part + 1) * count]
    inner = hist_low.shape[1]

    def with_first(rows, extra, hist):
        for slot in range(REB):
            extra = jnp.where(slots[:, : extra.shape[1]] == slot, hist[slot : slot + 1, :], extra)
        return jnp.concatenate([rows[:count] + extra, rows[count:]], axis=0)

    received = with_first(a_r[...], block(0), hist_first[0])
    keys = with_first(a_k[...], block(1), hist_first[1])
    values = with_first(a_v[...], block(2), hist_first[2])
    low = jnp.tanh(with_first(a_l[...], block(6)[:, :inner], hist_low[...])).astype(BF16)
    up_first[...] = jnp.concatenate([block(3), block(4), block(5), block(6)[:, channels // 2 :]], axis=1)
    decay = jnp.exp(-jnp.exp(base[...] + dot(low, w_right[...])))
    occ = column_of(plan, OCCUPIED, count, channels)
    slot_of = lambda rows: [rows[slot * count : (slot + 1) * count] for slot in range(4)]
    r, k, v, d = slot_of(received), slot_of(keys), slot_of(values), slot_of(decay)
    d = [jnp.where(occ > slot, d[slot], 1.0) for slot in range(4)]
    k_live = [jnp.where(occ > slot, k[slot], 0.0) for slot in range(4)]
    before = [jnp.ones_like(d[0])]
    for slot in range(4):
        before.append(before[-1] * d[slot])
    query = jnp.concatenate([r[slot] * before[slot] for slot in range(4)], axis=0)
    scores, pairs = [], []
    for slot in range(4):
        scores.append(r[slot] * reward[...] * k[slot])
        pairs.append((slot, slot))
        between = jnp.ones_like(d[0])
        for earlier in range(slot - 1, -1, -1):
            scores.append(r[slot] * between * k_live[earlier])
            pairs.append((slot, earlier))
            between = between * d[earlier]
    sums = head_sums(jnp.concatenate(scores, axis=0))
    inner = [jnp.zeros_like(v[0])] * 4
    for index, (slot, earlier) in enumerate(pairs):
        inner[slot] = inner[slot] + sums[index * count : (index + 1) * count] * v[earlier]
    mixed = jnp.concatenate(inner, axis=0)
    after = jnp.ones_like(d[0])
    k_after = [None] * 4
    for slot in range(3, -1, -1):
        k_after[slot] = k_live[slot] * after
        after = after * d[slot]
    k_high, k_low = halves(jnp.concatenate(k_after, axis=0))
    v_high, v_low = halves(values)
    k_rows = jnp.concatenate([k_high, k_high, k_low], axis=0)
    v_rows = jnp.concatenate([v_high, v_low, v_high], axis=0).astype(F32)
    k_columns = jnp.transpose(k_rows.astype(F32)).astype(BF16)
    after_columns = jnp.transpose(before[4])
    q_high, q_low = halves(query)
    q_rows = jnp.concatenate([q_high, q_low], axis=0).astype(F32)
    q_request = iota(q_rows.shape, 0) % count
    v_request = iota(v_rows.shape, 0) % count
    blocks = head_blocks(channels)
    total = jnp.zeros((q_rows.shape[0], channels), F32)
    for index in range(count):
        packed = moved[pl.ds(index * WIDTH, WIDTH), :].astype(F32)
        for slot in range(REB):
            packed = jnp.where(place[index] == slot, rebuilt[slot], packed)
        tall = jnp.concatenate([packed] * (channels // WIDTH), axis=0)
        tall = jnp.where(blocks, tall, 0.0).astype(BF16)
        total = total + dot(jnp.where(q_request == index, q_rows, 0.0).astype(BF16), tall)
        update = dot(k_columns, jnp.where(v_request == index, v_rows, 0.0).astype(BF16))
        for which in range(channels // WIDTH):
            rows = slice(which * WIDTH, (which + 1) * WIDTH)
            lanes = slice(which // 2 * 128, which // 2 * 128 + 128)
            block = update[rows, lanes] + after_columns[rows, index : index + 1] * packed[:, lanes]
            if which % 2:
                block = pltpu.roll(block, 64, 1)
            next_state[index, which] = block[:, :WIDTH]
    mixed = mixed + total[: 4 * count] + total[4 * count :]
    centered = mixed - head_sums(mixed) * (1.0 / WIDTH)
    spread = head_sums(centered * centered) * (1.0 / WIDTH)
    heads_out = (centered * lax.rsqrt(spread + EPSILON) * gain[...]).astype(BF16)
    partial[...] = dot(heads_out, w_out[...]).astype(BF16)


def ffn_kernel(
    plan, own, by_one, by_two, by_three, p_own, p_one, p_two, p_three, up_first, gain, rates,
    w_up, w_down,
    kept, to_one, to_two, to_three, channel_last,
    entries,
):
    ranks = 4
    feature = own.shape[1]
    tokens = p_own.shape[0]
    count = tokens // 4
    hist_rows = REB * 32
    me = lax.axis_index("head")
    for steps, piece in enumerate((own, by_one, by_two, by_three)):
        block = lax.rem(me - steps + ranks, ranks)
        entries[:, pl.ds(pl.multiple_of(block * feature, feature), feature)] = piece[
            pl.ds(hist_rows, tokens), :
        ].astype(F32)
    mix = sum(piece[...].astype(F32) for piece in (p_own, p_one, p_two, p_three))
    middle = (entries[...] + mix).astype(BF16).astype(F32)
    entries[...] = middle
    own_lanes = pl.ds(pl.multiple_of(me * feature, feature), feature)
    middle_own = entries[:, own_lanes]
    current = normalize(middle, gain[...])
    previous = jnp.concatenate([jnp.zeros_like(current[:count]), current[:-count]], axis=0)
    blended = (current + (previous - current) * rates[4:5, :]).astype(BF16)
    hidden = dot(blended, w_up[...])
    hidden = jnp.concatenate([hidden[:count] + up_first[...], hidden[count:]], axis=0)
    hidden = jnp.maximum(hidden, 0.0)
    hidden = (hidden * hidden).astype(BF16)
    for steps, target in enumerate((kept, to_one, to_two, to_three)):
        block = lax.rem(me + steps, ranks)
        lanes = pl.ds(pl.multiple_of(block * feature, feature), feature)
        rows = dot(hidden, w_down[:, lanes])
        if steps == 0:
            target[...] = rows + middle_own
        else:
            target[...] = rows.astype(BF16)
    occ = column_of(plan, OCCUPIED, count, current.shape[1])
    last = jnp.zeros((count, current.shape[1]), F32)
    for slot in range(4):
        last = jnp.where(occ == slot + 1, current[slot * count : (slot + 1) * count], last)
    entries[pl.ds(0, count), :] = last
    channel_last[...] = entries[pl.ds(0, count), own_lanes]


def on_device(
    arriving_hiddens,
    occupied_slot_totals,
    former_indices,
    reconstruct_marks,
    retained_hiddens,
    carried_memory_matrices,
    lagged_previous_entries,
    pre_attention_scaling,
    pre_feedforward_scaling,
    lag_blend_fractions,
    acceptance_projection,
    address_projection,
    content_projection,
    fading_lowrank_left,
    fading_lowrank_right,
    fading_baseline_entries,
    present_item_reward,
    grouped_layer_scaling,
    attention_exit_projection,
    feedforward_address_proj,
    feedforward_content_proj,
):
    count, steps, feature = arriving_hiddens.shape
    heads = carried_memory_matrices.shape[1]
    channels = heads * WIDTH
    hist = retained_hiddens.shape[1]
    model = pre_attention_scaling.shape[0]
    tokens = count * steps
    row = lambda value: value.reshape(1, -1)
    home, seated, aux_rows = count * WIDTH, SEATS * WIDTH, AUX * count
    far_weights = (
        acceptance_projection,
        address_projection,
        content_projection,
        fading_lowrank_left.T,
    )
    gathered, plus, minus, stay, *weights, plan = call(
        pack_kernel,
        "pack",
        (
            out((REB * hist + tokens + 2 * count, feature), BF16),
            out((seated, channels), BF16),
            out((seated, channels), BF16),
            out((home, channels), BF16),
            *(out(value.shape, BF16) for value in far_weights),
            out((PLAN,), jnp.int32),
        ),
        [
            (former_indices, "scalars"),
            (reconstruct_marks, "scalars"),
            (occupied_slot_totals, "scalars"),
            (retained_hiddens, "any"),
            (carried_memory_matrices, "any"),
            (lagged_previous_entries, "load"),
            (arriving_hiddens, "load"),
            *((value, "any") for value in far_weights),
        ],
        [
            pltpu.VMEM((tokens + 2 * count, feature), F32),
            pltpu.VMEM((count, heads, WIDTH, WIDTH), F32),
            pltpu.SemaphoreType.DMA((REB,)),
            pltpu.SemaphoreType.DMA((count,)),
            pltpu.SemaphoreType.DMA((len(far_weights),)),
        ],
        (VMEM_SPEC,) * (4 + len(far_weights)) + (SMEM_SPEC,),
    )

    def send(stage, up, down):
        return rotate(up, "grp", -STRIDES[stage]), rotate(down, "grp", STRIDES[stage])

    plus, minus = send(0, plus, minus)
    pieces = [gathered] + [rotate(gathered, "head", k) for k in (1, 2, 3)]
    base = row(fading_baseline_entries)
    inner = fading_lowrank_left.shape[1]
    a_r, a_k, a_v, a_l, rebuilt, aux, hist_first, hist_low, time_last = call(
        project_kernel,
        "project",
        (
            out((tokens, channels), F32),
            out((tokens, channels), F32),
            out((tokens, channels), F32),
            out((tokens, inner), F32),
            out((REB, WIDTH, channels), F32),
            out((AUX * count, channels), BF16),
            out((3, count, channels), F32),
            out((count, inner), F32),
            out((count, feature), F32),
        ),
        [(plan, "smem")]
        + [(value, "vmem") for value in pieces]
        + [(row(pre_attention_scaling), "load"), (lag_blend_fractions, "load")]
        + [(value, "vmem") for value in weights]
        + [(feedforward_address_proj, "any"), (fading_lowrank_right, "load"), (base, "load")],
        [
            pltpu.VMEM((REB * hist + tokens + 2 * count, model), F32),
            pltpu.VMEM(feedforward_address_proj.shape, BF16),
            pltpu.SemaphoreType.DMA((1,)),
        ],
        cost=pl.CostEstimate(flops=20_000_000_000, transcendentals=0, bytes_accessed=8_000_000),
    )
    arrived = (plus, minus, stay, *send(0, aux, aux), aux)
    shape = lambda rows: out((rows + aux_rows, channels), BF16)
    for stage in range(STAGES):
        last = stage + 1 == STAGES
        merged = call(
            functools.partial(merge_kernel, stage, count, stage == 0),
            "merge",
            shape(home) if last else (shape(seated), shape(seated), shape(home)),
            [(plan, "smem")] + [(value, "vmem") for value in arrived],
            [] if last else [pltpu.VMEM((home, channels), BF16)],
        )
        if not last:
            arrived = (*send(stage + 1, *merged[:2]), merged[2])

    def move_all(moved, aux, plan, former, state):
        packed = call(
            pack_all_kernel,
            "pack_all",
            out((home, channels), BF16),
            [(former, "scalars"), (state, "any")],
            [pltpu.VMEM((count, heads, WIDTH, WIDTH), F32), pltpu.SemaphoreType.DMA((count,))],
        )
        moved = jnp.concatenate([packed, aux], axis=0)
        for stage in range(STAGES):
            moved = call(
                functools.partial(merge_all_kernel, stage, count),
                "merge_all",
                shape(home),
                [(plan, "smem")] + [(value, "load") for value in (*send(stage, moved, moved), moved)],
            )
        return moved

    moved = lax.cond(
        plan[OVER] > 0,
        move_all,
        lambda moved, *_: moved,
        merged,
        aux,
        plan,
        former_indices,
        carried_memory_matrices,
    )
    next_state, partial, up_first = call(
        recur_kernel,
        "recur",
        (
            out((count, heads, WIDTH, WIDTH), F32),
            out((tokens, model), BF16),
            out((count, feedforward_address_proj.shape[1]), F32),
        ),
        [(plan, "smem")]
        + [(value, "vmem") for value in (moved, hist_first, hist_low, rebuilt, a_r, a_k, a_v, a_l)]
        + [(fading_lowrank_right, "load"), (base, "load")]
        + [(row(present_item_reward), "load"), (row(grouped_layer_scaling), "load")]
        + [(attention_exit_projection, "vmem")],
    )
    partials = [partial] + [rotate(partial, "head", k) for k in (1, 2, 3)]
    ffn_weights, _ = lax.optimization_barrier(
        ((feedforward_address_proj, feedforward_content_proj), partial)
    )
    ffn_weights = call(
        fetch_kernel,
        "fetch",
        tuple(out(value.shape, BF16) for value in ffn_weights),
        [(value, "any") for value in ffn_weights],
        [pltpu.SemaphoreType.DMA((len(ffn_weights),))],
    )
    kept, to_one, to_two, to_three, channel_last = call(
        ffn_kernel,
        "ffn",
        (
            out((tokens, feature), F32),
            out((tokens, feature), BF16),
            out((tokens, feature), BF16),
            out((tokens, feature), BF16),
            out((count, feature), F32),
        ),
        [(plan, "smem")]
        + [(value, "vmem") for value in (*pieces, *partials, up_first)]
        + [(row(pre_feedforward_scaling), "load"), (lag_blend_fractions, "load")]
        + [(value, "vmem") for value in ffn_weights],
        [pltpu.VMEM((tokens, model), F32)],
    )
    arrived = [rotate(value, "head", k + 1) for k, value in enumerate((to_one, to_two, to_three))]
    result = kept + sum(value.astype(F32) for value in arrived)
    result = jnp.swapaxes(result.astype(BF16).reshape(steps, count, feature), 0, 1)
    valid_rows = jnp.arange(steps)[None, :] < occupied_slot_totals[:, None]
    result = jnp.where(valid_rows[..., None], result, jnp.zeros_like(result))
    return (result, next_state, jnp.stack([time_last, channel_last], axis=1))


def solution(mesh):
    placed = (
        P("grp", None, "head"),
        P("grp"),
        P("grp"),
        P("grp"),
        P("grp", None, "head"),
        P("grp", "head", None, None),
        P("grp", None, "head"),
        P(),
        P(),
        P(),
        P(None, "head"),
        P(None, "head"),
        P(None, "head"),
        P(),
        P(None, "head"),
        P("head"),
        P("head"),
        P("head"),
        P("head", None),
        P(None, "head"),
        P("head", None),
    )
    return jax.shard_map(
        on_device,
        mesh=mesh,
        in_specs=placed,
        out_specs=(P("grp", None, "head"), P("grp", "head", None, None), P("grp", None, "head")),
        check_vma=False,
    )
```

```python
import functools

import jax
import jax.numpy as jnp
from jax import lax
from jax.experimental import pallas as pl
from jax.experimental.pallas import tpu as pltpu
from jax.sharding import PartitionSpec as P

WIDTH = 64
REB = 2
EPSILON = 1e-05
F32 = jnp.float32
BF16 = jnp.bfloat16
HIGH = lax.Precision.HIGHEST
VMEM_LIMIT = 40 * 1024 * 1024
SMEM_SPEC = pl.BlockSpec(memory_space=pltpu.SMEM)
VMEM_SPEC = pl.BlockSpec(memory_space=pltpu.VMEM)
ANY_SPEC = pl.BlockSpec(memory_space=pl.ANY)


def rotate(value, axis, steps):
    count = lax.axis_size(axis)
    pairs = [(source, (source + steps) % count) for source in range(count)]
    return lax.ppermute(value, axis, pairs)


def on_chip(value):
    return pltpu.with_memory_space_constraint(value, pltpu.VMEM)


def off_chip(value):
    return pltpu.with_memory_space_constraint(value, pltpu.HBM)


SPECS = {"smem": SMEM_SPEC, "vmem": VMEM_SPEC, "load": VMEM_SPEC, "any": ANY_SPEC, "scalars": SMEM_SPEC}
PLACES = {"vmem": on_chip, "load": off_chip, "any": off_chip, "scalars": off_chip}


def call(kernel, name, out_shape, operands, scratch=(), out_specs=None, cost=None):
    return pl.pallas_call(
        kernel,
        name=name,
        out_shape=out_shape,
        in_specs=[SPECS[place] for _, place in operands],
        out_specs=jax.tree.map(lambda _: VMEM_SPEC, out_shape) if out_specs is None else out_specs,
        scratch_shapes=list(scratch),
        cost_estimate=cost,
        compiler_params=pltpu.CompilerParams(vmem_limit_bytes=VMEM_LIMIT),
    )(*[PLACES.get(place, lambda value: value)(array) for array, place in operands])


def out(shape, dtype):
    return jax.ShapeDtypeStruct(shape, dtype)


def normalize(rows, gain):
    centered = rows - jnp.mean(rows, axis=-1, keepdims=True)
    spread = jnp.mean(centered * centered, axis=-1, keepdims=True)
    return (centered * lax.rsqrt(spread + EPSILON) * gain).astype(BF16).astype(F32)


def dot(left, right, contract=(1, 0), precision=None):
    return lax.dot_general(
        left,
        right,
        (((contract[0],), (contract[1],)), ((), ())),
        precision=precision,
        preferred_element_type=F32,
    )


def halves(value):
    high = value.astype(BF16)
    return high, (value - high.astype(F32)).astype(BF16)


def iota(shape, axis):
    return lax.broadcasted_iota(jnp.int32, shape, axis)


def column_of(plan, base, rows, lanes):
    row = iota((rows, lanes), 0)
    result = jnp.zeros((rows, lanes), jnp.int32)
    for index in range(rows):
        result = jnp.where(row == index, plan[base + index], result)
    return result


def head_blocks(lanes):
    return iota((lanes, lanes), 0) // WIDTH == iota((lanes, lanes), 1) // WIDTH


def head_sums(rows):
    ones = head_blocks(rows.shape[1]).astype(BF16)
    high, low = halves(rows)
    return dot(high, ones) + dot(low, ones)


STRIDES = (24, 3, 8, 1)
SEATS = 5
STAGES = len(STRIDES)
DIGIT, SEAT, PLACE, OCCUPIED, OVER, PLAN = 0, 32, 64, 72, 80, 88
AUX = 7


def signed_residue(value):
    residue = lax.rem(value, 8)
    return jnp.where(residue > 4, residue - 8, residue)


def plan_moves(former, plan, count):
    groups = lax.axis_size("grp")
    here = lax.axis_index("grp")
    distances = [
        lax.rem(lax.div(former[index], count) - here + groups, groups) for index in range(count)
    ]
    one = lambda test: test.astype(jnp.int32)
    over = jnp.int32(0)
    for far, near in ((1, 3), (0, 2)):
        values = [signed_residue(distance) for distance in distances]
        far_up = sum(one((value == 2) | (value == 3)) for value in values)
        far_down = sum(one((value == -2) | (value == -3)) for value in values)
        near_up = sum(one((value == 1) | (value == -2)) for value in values)
        near_down = sum(one((value == -1) | (value == 2)) for value in values)
        up, down = jnp.maximum(far_up, near_up), jnp.maximum(far_down, near_down)
        seats = {(far, 1): 0, (far, -1): 0, (near, 1): 0, (near, -1): 0}
        for index, value in enumerate(values):
            free = value == 4
            rise = free & (up <= down)
            fall = free & (up > down)
            up, down = up + one(rise), down + one(fall)
            value = jnp.where(fall, -4, value)
            distances[index] = lax.div(distances[index] - value + groups, 8)
            triple = one(value >= 2) - one(value <= -2)
            for stage, digit in ((far, triple), (near, value - 3 * triple)):
                plan[DIGIT + stage * count + index] = digit
                seat = jnp.where(digit == 1, seats[stage, 1], seats[stage, -1])
                plan[SEAT + stage * count + index] = jnp.minimum(seat, SEATS - 1)
                for sign in (1, -1):
                    seats[stage, sign] = seats[stage, sign] + one(digit == sign)
        for used in seats.values():
            over = jnp.maximum(over, one(used > SEATS))
    plan[OVER] = over


def seat_rows(plan, stage, index, count):
    seat = plan[SEAT + stage * count + index]
    return pl.ds(pl.multiple_of(seat * WIDTH, WIDTH), WIDTH)


def home_rows(index):
    return pl.ds(index * WIDTH, WIDTH)


def store_row(plan, stage, index, count, value, plus, minus, stay):
    digit = plan[DIGIT + stage * count + index]
    seat = seat_rows(plan, stage, index, count)
    for sign, target, rows in ((1, plus, seat), (-1, minus, seat), (0, stay, home_rows(index))):

        @pl.when(digit == sign)
        def _(target=target, rows=rows):
            target[rows, :] = value()


def load_row(plan, stage, index, count, target, plus, minus, stay):
    digit = plan[DIGIT + stage * count + index]
    seat = seat_rows(plan, stage, index, count)
    rows = home_rows(index)
    came = jnp.where(digit == 1, plus[seat, :], minus[seat, :])
    target[rows, :] = jnp.where(digit == 0, stay[rows, :], came)


def pack_kernel(
    former, marks, occupied, held, state, shifts, tokens, far_r, far_k, far_v, far_left,
    gathered, plus, minus, stay, w_r, w_k, w_v, w_left, plan,
    slots, rows, sems, row_sems, weight_sems,
):
    count, heads = rows.shape[0], rows.shape[1]
    hist = held.shape[1]
    sources = [lax.rem(former[index], count) for index in range(count)]
    row_copies = [
        pltpu.make_async_copy(state.at[source], rows.at[index], row_sems.at[index])
        for index, source in enumerate(sources)
    ]
    for copy in row_copies:
        copy.start()
    far = (far_r, far_k, far_v, far_left)
    weight_copies = [
        pltpu.make_async_copy(source, target, weight_sems.at[index])
        for index, (source, target) in enumerate(zip(far, (w_r, w_k, w_v, w_left)))
    ]
    for copy in weight_copies:
        copy.start()
    rank = jnp.int32(0)
    chosen = [jnp.int32(0)] * REB
    for index in range(count):
        marked = marks[index] == 1
        chosen = [
            jnp.where(marked & (rank == place), index, value) for place, value in enumerate(chosen)
        ]
        plan[PLACE + index] = jnp.where(marked, rank, REB)
        rank = rank + marks[index]
        plan[OCCUPIED + index] = occupied[index]
    copies = [
        pltpu.make_async_copy(held.at[value], gathered.at[pl.ds(place * hist, hist)], sems.at[place])
        for place, value in enumerate(chosen)
    ]
    for copy in copies:
        copy.start()
    plan_moves(former, plan, count)
    base = REB * hist
    for index in range(count):
        lines = tokens[index].astype(F32)
        for slot in range(4):
            slots[slot * count + index : slot * count + index + 1, :] = lines[slot : slot + 1]
        line = shifts[sources[index]]
        for which in range(2):
            row = (4 + which) * count + index
            slots[row : row + 1, :] = line[which : which + 1]
    gathered[pl.ds(base, slots.shape[0]), :] = slots[...].astype(BF16)
    for index in range(count):
        row_copies[index].wait()
        whole = rows[index]
        wide = jnp.concatenate([whole[head] for head in range(heads)], axis=1).astype(BF16)
        store_row(plan, 0, index, count, lambda: wide, plus, minus, stay)
    for copy in copies + weight_copies:
        copy.wait()


def pack_all_kernel(former, state, packed, rows, row_sems):
    count, heads = rows.shape[0], rows.shape[1]
    row_copies = [
        pltpu.make_async_copy(state.at[lax.rem(former[index], count)], rows.at[index], row_sems.at[index])
        for index in range(count)
    ]
    for copy in row_copies:
        copy.start()
    for index in range(count):
        row_copies[index].wait()
        whole = rows[index]
        wide = jnp.concatenate([whole[head] for head in range(heads)], axis=1)
        packed[home_rows(index), :] = wide.astype(BF16)


def pick_aux(plan, stage, plus, minus, stay, count):
    shape = (count, plus.shape[1])
    request = iota(shape, 0)
    take = jnp.zeros(shape, jnp.int32)
    for index in range(count):
        take = jnp.where(request == index, plan[DIGIT + stage * count + index], take)
    take = jnp.concatenate([take] * (plus.shape[0] // count), axis=0)
    plus, minus, stay = (value.astype(F32) for value in (plus, minus, stay))
    return jnp.where(take == 1, plus, jnp.where(take == -1, minus, stay)).astype(BF16)


def merge_kernel(stage, count, separate, plan, *refs):
    plus, minus, stay = refs[:3]
    seated, home = SEATS * WIDTH, count * WIDTH
    aux = AUX * count
    if separate:
        aux_values = [ref[...] for ref in refs[3:6]]
        refs = refs[6:]
    else:
        aux_values = [plus[pl.ds(seated, aux), :], minus[pl.ds(seated, aux), :], stay[pl.ds(home, aux), :]]
        refs = refs[3:]
    picked = pick_aux(plan, stage, *aux_values, count)
    if stage + 1 == STAGES:
        (moved,) = refs
        for index in range(count):
            load_row(plan, stage, index, count, moved, plus, minus, stay)
        moved[pl.ds(home, aux), :] = picked
        return
    next_plus, next_minus, next_stay, hold = refs
    for index in range(count):
        load_row(plan, stage, index, count, hold, plus, minus, stay)
    for index in range(count):
        rows = home_rows(index)
        store_row(plan, stage + 1, index, count, lambda: hold[rows, :], next_plus, next_minus, next_stay)
    next_plus[pl.ds(seated, aux), :] = picked
    next_minus[pl.ds(seated, aux), :] = picked
    next_stay[pl.ds(home, aux), :] = picked


def merge_all_kernel(stage, count, plan, plus, minus, stay, moved):
    home, aux = count * WIDTH, AUX * count
    for index in range(count):
        digit = plan[DIGIT + stage * count + index]
        rows = home_rows(index)
        for sign, source in ((1, plus), (-1, minus), (0, stay)):

            @pl.when(digit == sign)
            def _(source=source, rows=rows):
                moved[rows, :] = source[rows, :]

    tail = pl.ds(home, aux)
    moved[tail, :] = pick_aux(plan, stage, plus[tail, :], minus[tail, :], stay[tail, :], count)


def fetch_kernel(*refs):
    count = (len(refs) - 1) // 2
    copies = [
        pltpu.make_async_copy(far, near, refs[-1].at[index])
        for index, (far, near) in enumerate(zip(refs[:count], refs[count:-1]))
    ]
    for copy in copies:
        copy.start()
    for copy in copies:
        copy.wait()


def project_kernel(
    plan, own, by_one, by_two, by_three, gain, rates, w_r, w_k, w_v, w_left, far_up, w_right, base,
    a_r, a_k, a_v, a_l, rebuilt, aux, hist_first, hist_low, time_last,
    entries, w_up, up_sem,
):
    fetch_up = pltpu.make_async_copy(far_up, w_up, up_sem.at[0])
    fetch_up.start()
    ranks = 4
    feature = own.shape[1]
    hist_rows = REB * 32
    tokens = a_r.shape[0]
    count = tokens // 4
    normal = hist_rows + tokens
    me = lax.axis_index("head")
    for steps, piece in enumerate((own, by_one, by_two, by_three)):
        block = lax.rem(me - steps + ranks, ranks)
        entries[:, pl.ds(pl.multiple_of(block * feature, feature), feature)] = piece[...].astype(F32)
    current = normalize(entries[pl.ds(0, normal), :], gain[...])
    hist = current[:hist_rows]
    live = current[hist_rows:]
    place = iota(hist.shape, 0) % 32
    hist_previous = jnp.where(place == 0, 0.0, pltpu.roll(hist, 1, 0))
    live_previous = jnp.concatenate([jnp.zeros_like(live[:count]), live[:-count]], axis=0)
    previous = jnp.concatenate([hist_previous, live_previous], axis=0)
    change = previous - current
    moved_shift = entries[pl.ds(normal, count), :]
    lines = iota(moved_shift.shape, 0)
    last_hist = jnp.zeros_like(moved_shift)
    for slot in range(REB):
        last_hist = jnp.where(lines == slot, hist[slot * 32 + 31 : slot * 32 + 32], last_hist)
    first = jnp.concatenate([moved_shift, last_hist], axis=0)

    def mixed(which):
        rate = rates[which : which + 1, :]
        return jnp.concatenate([current + change * rate, first * rate], axis=0).astype(BF16)

    keys = dot(mixed(1), w_k[...])
    values = dot(mixed(2), w_v[...])
    low = dot(mixed(3), w_left[...], (1, 1))
    received = dot(mixed(0)[hist_rows:], w_r[...])
    a_r[...] = received[:tokens]
    a_k[...] = keys[hist_rows:normal]
    a_v[...] = values[hist_rows:normal]
    a_l[...] = low[hist_rows:normal]
    hist_first[0] = received[tokens + count :]
    hist_first[1] = keys[normal + count :]
    hist_first[2] = values[normal + count :]
    hist_low[...] = low[normal + count :]
    moving = [received[tokens : tokens + count], keys[normal : normal + count], values[normal : normal + count]]
    low_moving = low[normal : normal + count]
    keys, values, low = keys[:hist_rows], values[:hist_rows], low[:hist_rows]
    rank = jnp.tanh(low).astype(BF16)
    decay = jnp.exp(-jnp.exp(base[...] + dot(rank, w_right[...])))
    spot = iota(decay.shape, 0) % 32
    product = decay
    for steps in (1, 2, 4, 8, 16):
        product = product * jnp.where(spot + steps < 32, pltpu.roll(product, hist_rows - steps, 0), 1.0)
    later = jnp.where(spot < 31, pltpu.roll(product, hist_rows - 1, 0), 1.0)
    keys = keys * later
    lane = iota((WIDTH, values.shape[1]), 1) // WIDTH
    for slot in range(REB):
        span = slice(slot * 32, slot * 32 + 32)
        k_high, k_low = halves(keys[span])
        v_high, v_low = halves(values[span])
        outer = dot(
            jnp.concatenate([k_high, k_high, k_low], axis=0),
            jnp.concatenate([v_high, v_low, v_high], axis=0),
            (0, 0),
        )
        packed = outer[:WIDTH]
        for which in range(1, values.shape[1] // WIDTH):
            packed = jnp.where(lane == which, outer[which * WIDTH : (which + 1) * WIDTH], packed)
        rebuilt[slot] = packed
    fetch_up.wait()
    up = dot((entries[pl.ds(normal + count, count), :] * rates[4:5, :]).astype(BF16), w_up[...])
    lanes = aux.shape[1]
    whole = up.shape[1] // lanes
    left = jnp.concatenate([low_moving, jnp.zeros((count, lanes // 2 - low_moving.shape[1]), F32)], axis=1)
    moving += [up[:, part * lanes : (part + 1) * lanes] for part in range(whole)]
    moving += [jnp.concatenate([left, up[:, whole * lanes :]], axis=1)]
    aux[...] = jnp.concatenate(moving, axis=0).astype(BF16)
    occ = column_of(plan, OCCUPIED, count, current.shape[1])
    last = jnp.zeros((count, current.shape[1]), F32)
    for slot in range(4):
        last = jnp.where(occ == slot + 1, live[slot * count : (slot + 1) * count], last)
    entries[pl.ds(0, count), :] = last
    time_last[...] = entries[pl.ds(0, count), pl.ds(pl.multiple_of(me * feature, feature), feature)]


def recur_kernel(
    plan, moved, hist_first, hist_low, rebuilt, a_r, a_k, a_v, a_l, w_right, base, reward, gain, w_out,
    next_state, partial, up_first,
):
    count = next_state.shape[0]
    channels = a_r.shape[1]
    place = [plan[PLACE + index] for index in range(count)]
    slots = column_of(plan, PLACE, count, channels)
    aux = moved[pl.ds(count * WIDTH, AUX * count), :].astype(F32)
    block = lambda part: aux[part * count : (part + 1) * count]
    inner = hist_low.shape[1]

    def with_first(rows, extra, hist):
        for slot in range(REB):
            extra = jnp.where(slots[:, : extra.shape[1]] == slot, hist[slot : slot + 1, :], extra)
        return jnp.concatenate([rows[:count] + extra, rows[count:]], axis=0)

    received = with_first(a_r[...], block(0), hist_first[0])
    keys = with_first(a_k[...], block(1), hist_first[1])
    values = with_first(a_v[...], block(2), hist_first[2])
    low = jnp.tanh(with_first(a_l[...], block(6)[:, :inner], hist_low[...])).astype(BF16)
    up_first[...] = jnp.concatenate([block(3), block(4), block(5), block(6)[:, channels // 2 :]], axis=1)
    decay = jnp.exp(-jnp.exp(base[...] + dot(low, w_right[...])))
    occ = column_of(plan, OCCUPIED, count, channels)
    slot_of = lambda rows: [rows[slot * count : (slot + 1) * count] for slot in range(4)]
    r, k, v, d = slot_of(received), slot_of(keys), slot_of(values), slot_of(decay)
    d = [jnp.where(occ > slot, d[slot], 1.0) for slot in range(4)]
    k_live = [jnp.where(occ > slot, k[slot], 0.0) for slot in range(4)]
    before = [jnp.ones_like(d[0])]
    for slot in range(4):
        before.append(before[-1] * d[slot])
    query = jnp.concatenate([r[slot] * before[slot] for slot in range(4)], axis=0)
    scores, pairs = [], []
    for slot in range(4):
        scores.append(r[slot] * reward[...] * k[slot])
        pairs.append((slot, slot))
        between = jnp.ones_like(d[0])
        for earlier in range(slot - 1, -1, -1):
            scores.append(r[slot] * between * k_live[earlier])
            pairs.append((slot, earlier))
            between = between * d[earlier]
    sums = head_sums(jnp.concatenate(scores, axis=0))
    inner = [jnp.zeros_like(v[0])] * 4
    for index, (slot, earlier) in enumerate(pairs):
        inner[slot] = inner[slot] + sums[index * count : (index + 1) * count] * v[earlier]
    mixed = jnp.concatenate(inner, axis=0)
    after = jnp.ones_like(d[0])
    k_after = [None] * 4
    for slot in range(3, -1, -1):
        k_after[slot] = k_live[slot] * after
        after = after * d[slot]
    k_high, k_low = halves(jnp.concatenate(k_after, axis=0))
    v_high, v_low = halves(values)
    k_rows = jnp.concatenate([k_high, k_high, k_low], axis=0)
    v_rows = jnp.concatenate([v_high, v_low, v_high], axis=0).astype(F32)
    k_columns = jnp.transpose(k_rows.astype(F32)).astype(BF16)
    after_columns = jnp.transpose(before[4])
    q_high, q_low = halves(query)
    q_rows = jnp.concatenate([q_high, q_low], axis=0).astype(F32)
    q_request = iota(q_rows.shape, 0) % count
    v_request = iota(v_rows.shape, 0) % count
    blocks = head_blocks(channels)
    total = jnp.zeros((q_rows.shape[0], channels), F32)
    for index in range(count):
        packed = moved[pl.ds(index * WIDTH, WIDTH), :].astype(F32)
        for slot in range(REB):
            packed = jnp.where(place[index] == slot, rebuilt[slot], packed)
        tall = jnp.concatenate([packed] * (channels // WIDTH), axis=0)
        tall = jnp.where(blocks, tall, 0.0).astype(BF16)
        total = total + dot(jnp.where(q_request == index, q_rows, 0.0).astype(BF16), tall)
        update = dot(k_columns, jnp.where(v_request == index, v_rows, 0.0).astype(BF16))
        for which in range(channels // WIDTH):
            rows = slice(which * WIDTH, (which + 1) * WIDTH)
            lanes = slice(which // 2 * 128, which // 2 * 128 + 128)
            block = update[rows, lanes] + after_columns[rows, index : index + 1] * packed[:, lanes]
            if which % 2:
                block = pltpu.roll(block, 64, 1)
            next_state[index, which] = block[:, :WIDTH]
    mixed = mixed + total[: 4 * count] + total[4 * count :]
    centered = mixed - head_sums(mixed) * (1.0 / WIDTH)
    spread = head_sums(centered * centered) * (1.0 / WIDTH)
    heads_out = (centered * lax.rsqrt(spread + EPSILON) * gain[...]).astype(BF16)
    partial[...] = dot(heads_out, w_out[...]).astype(BF16)


def ffn_kernel(
    plan, own, by_one, by_two, by_three, p_own, p_one, p_two, p_three, up_first, gain, rates,
    w_up, w_down,
    kept, to_one, to_two, to_three, channel_last,
    entries,
):
    ranks = 4
    feature = own.shape[1]
    tokens = p_own.shape[0]
    count = tokens // 4
    hist_rows = REB * 32
    me = lax.axis_index("head")
    for steps, piece in enumerate((own, by_one, by_two, by_three)):
        block = lax.rem(me - steps + ranks, ranks)
        entries[:, pl.ds(pl.multiple_of(block * feature, feature), feature)] = piece[
            pl.ds(hist_rows, tokens), :
        ].astype(F32)
    mix = sum(piece[...].astype(F32) for piece in (p_own, p_one, p_two, p_three))
    middle = (entries[...] + mix).astype(BF16).astype(F32)
    entries[...] = middle
    own_lanes = pl.ds(pl.multiple_of(me * feature, feature), feature)
    middle_own = entries[:, own_lanes]
    current = normalize(middle, gain[...])
    previous = jnp.concatenate([jnp.zeros_like(current[:count]), current[:-count]], axis=0)
    blended = (current + (previous - current) * rates[4:5, :]).astype(BF16)
    hidden = dot(blended, w_up[...])
    hidden = jnp.concatenate([hidden[:count] + up_first[...], hidden[count:]], axis=0)
    hidden = jnp.maximum(hidden, 0.0)
    hidden = (hidden * hidden).astype(BF16)
    for steps, target in enumerate((kept, to_one, to_two, to_three)):
        block = lax.rem(me + steps, ranks)
        lanes = pl.ds(pl.multiple_of(block * feature, feature), feature)
        rows = dot(hidden, w_down[:, lanes])
        if steps == 0:
            target[...] = rows + middle_own
        else:
            target[...] = rows.astype(BF16)
    occ = column_of(plan, OCCUPIED, count, current.shape[1])
    last = jnp.zeros((count, current.shape[1]), F32)
    for slot in range(4):
        last = jnp.where(occ == slot + 1, current[slot * count : (slot + 1) * count], last)
    entries[pl.ds(0, count), :] = last
    channel_last[...] = entries[pl.ds(0, count), own_lanes]


def on_device(
    arriving_hiddens,
    occupied_slot_totals,
    former_indices,
    reconstruct_marks,
    retained_hiddens,
    carried_memory_matrices,
    lagged_previous_entries,
    pre_attention_scaling,
    pre_feedforward_scaling,
    lag_blend_fractions,
    acceptance_projection,
    address_projection,
    content_projection,
    fading_lowrank_left,
    fading_lowrank_right,
    fading_baseline_entries,
    present_item_reward,
    grouped_layer_scaling,
    attention_exit_projection,
    feedforward_address_proj,
    feedforward_content_proj,
):
    count, steps, feature = arriving_hiddens.shape
    heads = carried_memory_matrices.shape[1]
    channels = heads * WIDTH
    hist = retained_hiddens.shape[1]
    model = pre_attention_scaling.shape[0]
    tokens = count * steps
    row = lambda value: value.reshape(1, -1)
    home, seated, aux_rows = count * WIDTH, SEATS * WIDTH, AUX * count
    far_weights = (
        acceptance_projection,
        address_projection,
        content_projection,
        fading_lowrank_left.T,
    )
    gathered, plus, minus, stay, *weights, plan = call(
        pack_kernel,
        "pack",
        (
            out((REB * hist + tokens + 2 * count, feature), BF16),
            out((seated, channels), BF16),
            out((seated, channels), BF16),
            out((home, channels), BF16),
            *(out(value.shape, BF16) for value in far_weights),
            out((PLAN,), jnp.int32),
        ),
        [
            (former_indices, "scalars"),
            (reconstruct_marks, "scalars"),
            (occupied_slot_totals, "scalars"),
            (retained_hiddens, "any"),
            (carried_memory_matrices, "any"),
            (lagged_previous_entries, "load"),
            (arriving_hiddens, "load"),
            *((value, "any") for value in far_weights),
        ],
        [
            pltpu.VMEM((tokens + 2 * count, feature), F32),
            pltpu.VMEM((count, heads, WIDTH, WIDTH), F32),
            pltpu.SemaphoreType.DMA((REB,)),
            pltpu.SemaphoreType.DMA((count,)),
            pltpu.SemaphoreType.DMA((len(far_weights),)),
        ],
        (VMEM_SPEC,) * (4 + len(far_weights)) + (SMEM_SPEC,),
    )

    def send(stage, up, down):
        return rotate(up, "grp", -STRIDES[stage]), rotate(down, "grp", STRIDES[stage])

    plus, minus = send(0, plus, minus)
    pieces = [gathered] + [rotate(gathered, "head", k) for k in (1, 2, 3)]
    base = row(fading_baseline_entries)
    inner = fading_lowrank_left.shape[1]
    a_r, a_k, a_v, a_l, rebuilt, aux, hist_first, hist_low, time_last = call(
        project_kernel,
        "project",
        (
            out((tokens, channels), F32),
            out((tokens, channels), F32),
            out((tokens, channels), F32),
            out((tokens, inner), F32),
            out((REB, WIDTH, channels), F32),
            out((AUX * count, channels), BF16),
            out((3, count, channels), F32),
            out((count, inner), F32),
            out((count, feature), F32),
        ),
        [(plan, "smem")]
        + [(value, "vmem") for value in pieces]
        + [(row(pre_attention_scaling), "load"), (lag_blend_fractions, "load")]
        + [(value, "vmem") for value in weights]
        + [(feedforward_address_proj, "any"), (fading_lowrank_right, "load"), (base, "load")],
        [
            pltpu.VMEM((REB * hist + tokens + 2 * count, model), F32),
            pltpu.VMEM(feedforward_address_proj.shape, BF16),
            pltpu.SemaphoreType.DMA((1,)),
        ],
        cost=pl.CostEstimate(flops=20_000_000_000, transcendentals=0, bytes_accessed=8_000_000),
    )
    arrived = (plus, minus, stay, *send(0, aux, aux), aux)
    shape = lambda rows: out((rows + aux_rows, channels), BF16)
    for stage in range(STAGES):
        last = stage + 1 == STAGES
        merged = call(
            functools.partial(merge_kernel, stage, count, stage == 0),
            "merge",
            shape(home) if last else (shape(seated), shape(seated), shape(home)),
            [(plan, "smem")] + [(value, "vmem") for value in arrived],
            [] if last else [pltpu.VMEM((home, channels), BF16)],
        )
        if not last:
            arrived = (*send(stage + 1, *merged[:2]), merged[2])

    def move_all(moved, aux, plan, former, state):
        packed = call(
            pack_all_kernel,
            "pack_all",
            out((home, channels), BF16),
            [(former, "scalars"), (state, "any")],
            [pltpu.VMEM((count, heads, WIDTH, WIDTH), F32), pltpu.SemaphoreType.DMA((count,))],
        )
        moved = jnp.concatenate([packed, aux], axis=0)
        for stage in range(STAGES):
            moved = call(
                functools.partial(merge_all_kernel, stage, count),
                "merge_all",
                shape(home),
                [(plan, "smem")] + [(value, "load") for value in (*send(stage, moved, moved), moved)],
            )
        return moved

    moved = lax.cond(
        plan[OVER] > 0,
        move_all,
        lambda moved, *_: moved,
        merged,
        aux,
        plan,
        former_indices,
        carried_memory_matrices,
    )
    next_state, partial, up_first = call(
        recur_kernel,
        "recur",
        (
            out((count, heads, WIDTH, WIDTH), F32),
            out((tokens, model), BF16),
            out((count, feedforward_address_proj.shape[1]), F32),
        ),
        [(plan, "smem")]
        + [(value, "vmem") for value in (moved, hist_first, hist_low, rebuilt, a_r, a_k, a_v, a_l)]
        + [(fading_lowrank_right, "load"), (base, "load")]
        + [(row(present_item_reward), "load"), (row(grouped_layer_scaling), "load")]
        + [(attention_exit_projection, "vmem")],
    )
    partials = [partial] + [rotate(partial, "head", k) for k in (1, 2, 3)]
    ffn_weights, _ = lax.optimization_barrier(
        ((feedforward_address_proj, feedforward_content_proj), partial)
    )
    ffn_weights = call(
        fetch_kernel,
        "fetch",
        tuple(out(value.shape, BF16) for value in ffn_weights),
        [(value, "any") for value in ffn_weights],
        [pltpu.SemaphoreType.DMA((len(ffn_weights),))],
    )
    kept, to_one, to_two, to_three, channel_last = call(
        ffn_kernel,
        "ffn",
        (
            out((tokens, feature), F32),
            out((tokens, feature), BF16),
            out((tokens, feature), BF16),
            out((tokens, feature), BF16),
            out((count, feature), F32),
        ),
        [(plan, "smem")]
        + [(value, "vmem") for value in (*pieces, *partials, up_first)]
        + [(row(pre_feedforward_scaling), "load"), (lag_blend_fractions, "load")]
        + [(value, "vmem") for value in ffn_weights],
        [pltpu.VMEM((tokens, model), F32)],
    )
    arrived = [rotate(value, "head", k + 1) for k, value in enumerate((to_one, to_two, to_three))]
    result = kept + sum(value.astype(F32) for value in arrived)
    result = jnp.swapaxes(result.astype(BF16).reshape(steps, count, feature), 0, 1)
    valid_rows = jnp.arange(steps)[None, :] < occupied_slot_totals[:, None]
    result = jnp.where(valid_rows[..., None], result, jnp.zeros_like(result))
    return (result, next_state, jnp.stack([time_last, channel_last], axis=1))


def solution(mesh):
    placed = (
        P("grp", None, "head"),
        P("grp"),
        P("grp"),
        P("grp"),
        P("grp", None, "head"),
        P("grp", "head", None, None),
        P("grp", None, "head"),
        P(),
        P(),
        P(),
        P(None, "head"),
        P(None, "head"),
        P(None, "head"),
        P(),
        P(None, "head"),
        P("head"),
        P("head"),
        P("head"),
        P("head", None),
        P(None, "head"),
        P("head", None),
    )
    return jax.shard_map(
        on_device,
        mesh=mesh,
        in_specs=placed,
        out_specs=(P("grp", None, "head"), P("grp", "head", None, None), P("grp", None, "head")),
        check_vma=False,
    )
```

```python
import functools

import jax
import jax.numpy as jnp
from jax import lax
from jax.experimental import pallas as pl
from jax.experimental.pallas import tpu as pltpu
from jax.sharding import PartitionSpec as P

WIDTH = 64
REB = 2
EPSILON = 1e-05
F32 = jnp.float32
BF16 = jnp.bfloat16
HIGH = lax.Precision.HIGHEST
VMEM_LIMIT = 40 * 1024 * 1024
SMEM_SPEC = pl.BlockSpec(memory_space=pltpu.SMEM)
VMEM_SPEC = pl.BlockSpec(memory_space=pltpu.VMEM)
ANY_SPEC = pl.BlockSpec(memory_space=pl.ANY)


def rotate(value, axis, steps):
    count = lax.axis_size(axis)
    pairs = [(source, (source + steps) % count) for source in range(count)]
    return lax.ppermute(value, axis, pairs)


def on_chip(value):
    return pltpu.with_memory_space_constraint(value, pltpu.VMEM)


def off_chip(value):
    return pltpu.with_memory_space_constraint(value, pltpu.HBM)


SPECS = {"smem": SMEM_SPEC, "vmem": VMEM_SPEC, "load": VMEM_SPEC, "any": ANY_SPEC, "scalars": SMEM_SPEC}
PLACES = {"vmem": on_chip, "load": off_chip, "any": off_chip, "scalars": off_chip}


def call(kernel, name, out_shape, operands, scratch=(), out_specs=None, cost=None):
    return pl.pallas_call(
        kernel,
        name=name,
        out_shape=out_shape,
        in_specs=[SPECS[place] for _, place in operands],
        out_specs=jax.tree.map(lambda _: VMEM_SPEC, out_shape) if out_specs is None else out_specs,
        scratch_shapes=list(scratch),
        cost_estimate=cost,
        compiler_params=pltpu.CompilerParams(vmem_limit_bytes=VMEM_LIMIT),
    )(*[PLACES.get(place, lambda value: value)(array) for array, place in operands])


def out(shape, dtype):
    return jax.ShapeDtypeStruct(shape, dtype)


def normalize(rows, gain):
    centered = rows - jnp.mean(rows, axis=-1, keepdims=True)
    spread = jnp.mean(centered * centered, axis=-1, keepdims=True)
    return (centered * lax.rsqrt(spread + EPSILON) * gain).astype(BF16).astype(F32)


def dot(left, right, contract=(1, 0), precision=None):
    return lax.dot_general(
        left,
        right,
        (((contract[0],), (contract[1],)), ((), ())),
        precision=precision,
        preferred_element_type=F32,
    )


def halves(value):
    high = value.astype(BF16)
    return high, (value - high.astype(F32)).astype(BF16)


def iota(shape, axis):
    return lax.broadcasted_iota(jnp.int32, shape, axis)


def column_of(plan, base, rows, lanes):
    row = iota((rows, lanes), 0)
    result = jnp.zeros((rows, lanes), jnp.int32)
    for index in range(rows):
        result = jnp.where(row == index, plan[base + index], result)
    return result


def head_blocks(lanes):
    return iota((lanes, lanes), 0) // WIDTH == iota((lanes, lanes), 1) // WIDTH


def head_sums(rows):
    ones = head_blocks(rows.shape[1]).astype(BF16)
    high, low = halves(rows)
    return dot(high, ones) + dot(low, ones)


STRIDES = (24, 3, 8, 1)
SEATS = 5
STAGES = len(STRIDES)
DIGIT, SEAT, PLACE, OCCUPIED, OVER, PLAN = 0, 32, 64, 72, 80, 88
AUX = 7


def signed_residue(value):
    residue = lax.rem(value, 8)
    return jnp.where(residue > 4, residue - 8, residue)


def plan_moves(former, plan, count):
    groups = lax.axis_size("grp")
    here = lax.axis_index("grp")
    distances = [
        lax.rem(lax.div(former[index], count) - here + groups, groups) for index in range(count)
    ]
    one = lambda test: test.astype(jnp.int32)
    over = jnp.int32(0)
    for far, near in ((1, 3), (0, 2)):
        values = [signed_residue(distance) for distance in distances]
        far_up = sum(one((value == 2) | (value == 3)) for value in values)
        far_down = sum(one((value == -2) | (value == -3)) for value in values)
        near_up = sum(one((value == 1) | (value == -2)) for value in values)
        near_down = sum(one((value == -1) | (value == 2)) for value in values)
        up, down = jnp.maximum(far_up, near_up), jnp.maximum(far_down, near_down)
        seats = {(far, 1): 0, (far, -1): 0, (near, 1): 0, (near, -1): 0}
        for index, value in enumerate(values):
            free = value == 4
            rise = free & (up <= down)
            fall = free & (up > down)
            up, down = up + one(rise), down + one(fall)
            value = jnp.where(fall, -4, value)
            distances[index] = lax.div(distances[index] - value + groups, 8)
            triple = one(value >= 2) - one(value <= -2)
            for stage, digit in ((far, triple), (near, value - 3 * triple)):
                plan[DIGIT + stage * count + index] = digit
                seat = jnp.where(digit == 1, seats[stage, 1], seats[stage, -1])
                plan[SEAT + stage * count + index] = jnp.minimum(seat, SEATS - 1)
                for sign in (1, -1):
                    seats[stage, sign] = seats[stage, sign] + one(digit == sign)
        for used in seats.values():
            over = jnp.maximum(over, one(used > SEATS))
    plan[OVER] = over


def seat_rows(plan, stage, index, count):
    seat = plan[SEAT + stage * count + index]
    return pl.ds(pl.multiple_of(seat * WIDTH, WIDTH), WIDTH)


def home_rows(index):
    return pl.ds(index * WIDTH, WIDTH)


def store_row(plan, stage, index, count, value, plus, minus, stay):
    digit = plan[DIGIT + stage * count + index]
    seat = seat_rows(plan, stage, index, count)
    for sign, target, rows in ((1, plus, seat), (-1, minus, seat), (0, stay, home_rows(index))):

        @pl.when(digit == sign)
        def _(target=target, rows=rows):
            target[rows, :] = value()


def arrived_row(plan, stage, index, count, plus, minus, stay):
    digit = plan[DIGIT + stage * count + index]
    seat = seat_rows(plan, stage, index, count)
    came = jnp.where(digit == 1, plus[seat, :], minus[seat, :])
    return jnp.where(digit == 0, stay[home_rows(index), :], came)


def pack_kernel(
    former, marks, occupied, held, state, shifts, tokens, far_r, far_k, far_v, far_left,
    gathered, plus, minus, stay, w_r, w_k, w_v, w_left, plan,
    slots, rows, sems, row_sems, weight_sems,
):
    count, heads = rows.shape[0], rows.shape[1]
    hist = held.shape[1]
    sources = [lax.rem(former[index], count) for index in range(count)]
    row_copies = [
        pltpu.make_async_copy(state.at[source], rows.at[index], row_sems.at[index])
        for index, source in enumerate(sources)
    ]
    for copy in row_copies:
        copy.start()
    far = (far_r, far_k, far_v, far_left)
    weight_copies = [
        pltpu.make_async_copy(source, target, weight_sems.at[index])
        for index, (source, target) in enumerate(zip(far, (w_r, w_k, w_v, w_left)))
    ]
    for copy in weight_copies:
        copy.start()
    rank = jnp.int32(0)
    chosen = [jnp.int32(0)] * REB
    for index in range(count):
        marked = marks[index] == 1
        chosen = [
            jnp.where(marked & (rank == place), index, value) for place, value in enumerate(chosen)
        ]
        plan[PLACE + index] = jnp.where(marked, rank, REB)
        rank = rank + marks[index]
        plan[OCCUPIED + index] = occupied[index]
    copies = [
        pltpu.make_async_copy(held.at[value], gathered.at[pl.ds(place * hist, hist)], sems.at[place])
        for place, value in enumerate(chosen)
    ]
    for copy in copies:
        copy.start()
    plan_moves(former, plan, count)
    base = REB * hist
    for index in range(count):
        lines = tokens[index].astype(F32)
        for slot in range(4):
            slots[slot * count + index : slot * count + index + 1, :] = lines[slot : slot + 1]
        line = shifts[sources[index]]
        for which in range(2):
            row = (4 + which) * count + index
            slots[row : row + 1, :] = line[which : which + 1]
    gathered[pl.ds(base, slots.shape[0]), :] = slots[...].astype(BF16)
    for index in range(count):
        row_copies[index].wait()
        whole = rows[index]
        wide = jnp.concatenate([whole[head] for head in range(heads)], axis=1).astype(BF16)
        store_row(plan, 0, index, count, lambda: wide, plus, minus, stay)
    for copy in copies + weight_copies:
        copy.wait()


def pack_all_kernel(former, state, packed, rows, row_sems):
    count, heads = rows.shape[0], rows.shape[1]
    row_copies = [
        pltpu.make_async_copy(state.at[lax.rem(former[index], count)], rows.at[index], row_sems.at[index])
        for index in range(count)
    ]
    for copy in row_copies:
        copy.start()
    for index in range(count):
        row_copies[index].wait()
        whole = rows[index]
        wide = jnp.concatenate([whole[head] for head in range(heads)], axis=1)
        packed[home_rows(index), :] = wide.astype(BF16)


def pick_aux(plan, stage, plus, minus, stay, count):
    shape = (count, plus.shape[1])
    request = iota(shape, 0)
    take = jnp.zeros(shape, jnp.int32)
    for index in range(count):
        take = jnp.where(request == index, plan[DIGIT + stage * count + index], take)
    take = jnp.concatenate([take] * (plus.shape[0] // count), axis=0)
    plus, minus, stay = (value.astype(F32) for value in (plus, minus, stay))
    return jnp.where(take == 1, plus, jnp.where(take == -1, minus, stay)).astype(BF16)


def merge_kernel(stage, count, separate, plan, *refs):
    plus, minus, stay = refs[:3]
    seated, home = SEATS * WIDTH, count * WIDTH
    aux = AUX * count
    if separate:
        aux_values = [ref[...] for ref in refs[3:6]]
        refs = refs[6:]
    else:
        aux_values = [plus[pl.ds(seated, aux), :], minus[pl.ds(seated, aux), :], stay[pl.ds(home, aux), :]]
        refs = refs[3:]
    picked = pick_aux(plan, stage, *aux_values, count)
    if stage + 1 == STAGES:
        (moved,) = refs
        for index in range(count):
            moved[home_rows(index), :] = arrived_row(plan, stage, index, count, plus, minus, stay)
        moved[pl.ds(home, aux), :] = picked
        return
    next_plus, next_minus, next_stay = refs
    for index in range(count):
        value = arrived_row(plan, stage, index, count, plus, minus, stay)
        store_row(plan, stage + 1, index, count, lambda: value, next_plus, next_minus, next_stay)
    next_plus[pl.ds(seated, aux), :] = picked
    next_minus[pl.ds(seated, aux), :] = picked
    next_stay[pl.ds(home, aux), :] = picked


def merge_all_kernel(stage, count, plan, plus, minus, stay, moved):
    home, aux = count * WIDTH, AUX * count
    for index in range(count):
        digit = plan[DIGIT + stage * count + index]
        rows = home_rows(index)
        for sign, source in ((1, plus), (-1, minus), (0, stay)):

            @pl.when(digit == sign)
            def _(source=source, rows=rows):
                moved[rows, :] = source[rows, :]

    tail = pl.ds(home, aux)
    moved[tail, :] = pick_aux(plan, stage, plus[tail, :], minus[tail, :], stay[tail, :], count)


def fetch_kernel(*refs):
    count = (len(refs) - 1) // 2
    copies = [
        pltpu.make_async_copy(far, near, refs[-1].at[index])
        for index, (far, near) in enumerate(zip(refs[:count], refs[count:-1]))
    ]
    for copy in copies:
        copy.start()
    for copy in copies:
        copy.wait()


def project_kernel(
    plan, own, by_one, by_two, by_three, gain, rates, w_r, w_k, w_v, w_left, far_up, w_right, base,
    a_r, a_k, a_v, a_l, rebuilt, aux, hist_first, hist_low, time_last,
    entries, w_up, up_sem,
):
    fetch_up = pltpu.make_async_copy(far_up, w_up, up_sem.at[0])
    fetch_up.start()
    ranks = 4
    feature = own.shape[1]
    hist_rows = REB * 32
    tokens = a_r.shape[0]
    count = tokens // 4
    normal = hist_rows + tokens
    me = lax.axis_index("head")
    for steps, piece in enumerate((own, by_one, by_two, by_three)):
        block = lax.rem(me - steps + ranks, ranks)
        entries[:, pl.ds(pl.multiple_of(block * feature, feature), feature)] = piece[...].astype(F32)
    current = normalize(entries[pl.ds(0, normal), :], gain[...])
    hist = current[:hist_rows]
    live = current[hist_rows:]
    place = iota(hist.shape, 0) % 32
    hist_previous = jnp.where(place == 0, 0.0, pltpu.roll(hist, 1, 0))
    live_previous = jnp.concatenate([jnp.zeros_like(live[:count]), live[:-count]], axis=0)
    previous = jnp.concatenate([hist_previous, live_previous], axis=0)
    change = previous - current
    moved_shift = entries[pl.ds(normal, count), :]
    lines = iota(moved_shift.shape, 0)
    last_hist = jnp.zeros_like(moved_shift)
    for slot in range(REB):
        last_hist = jnp.where(lines == slot, hist[slot * 32 + 31 : slot * 32 + 32], last_hist)
    first = jnp.concatenate([moved_shift, last_hist], axis=0)

    def mixed(which):
        rate = rates[which : which + 1, :]
        return jnp.concatenate([current + change * rate, first * rate], axis=0).astype(BF16)

    keys = dot(mixed(1), w_k[...])
    values = dot(mixed(2), w_v[...])
    low = dot(mixed(3), w_left[...], (1, 1))
    received = dot(mixed(0)[hist_rows:], w_r[...])
    a_r[...] = received[:tokens]
    a_k[...] = keys[hist_rows:normal]
    a_v[...] = values[hist_rows:normal]
    a_l[...] = low[hist_rows:normal]
    hist_first[0] = received[tokens + count :]
    hist_first[1] = keys[normal + count :]
    hist_first[2] = values[normal + count :]
    hist_low[...] = low[normal + count :]
    moving = [received[tokens : tokens + count], keys[normal : normal + count], values[normal : normal + count]]
    low_moving = low[normal : normal + count]
    keys, values, low = keys[:hist_rows], values[:hist_rows], low[:hist_rows]
    rank = jnp.tanh(low).astype(BF16)
    decay = jnp.exp(-jnp.exp(base[...] + dot(rank, w_right[...])))
    spot = iota(decay.shape, 0) % 32
    product = decay
    for steps in (1, 2, 4, 8, 16):
        product = product * jnp.where(spot + steps < 32, pltpu.roll(product, hist_rows - steps, 0), 1.0)
    later = jnp.where(spot < 31, pltpu.roll(product, hist_rows - 1, 0), 1.0)
    keys = keys * later
    lane = iota((WIDTH, values.shape[1]), 1) // WIDTH
    for slot in range(REB):
        span = slice(slot * 32, slot * 32 + 32)
        k_high, k_low = halves(keys[span])
        v_high, v_low = halves(values[span])
        outer = dot(
            jnp.concatenate([k_high, k_high, k_low], axis=0),
            jnp.concatenate([v_high, v_low, v_high], axis=0),
            (0, 0),
        )
        packed = outer[:WIDTH]
        for which in range(1, values.shape[1] // WIDTH):
            packed = jnp.where(lane == which, outer[which * WIDTH : (which + 1) * WIDTH], packed)
        rebuilt[slot] = packed
    fetch_up.wait()
    up = dot((entries[pl.ds(normal + count, count), :] * rates[4:5, :]).astype(BF16), w_up[...])
    lanes = aux.shape[1]
    whole = up.shape[1] // lanes
    left = jnp.concatenate([low_moving, jnp.zeros((count, lanes // 2 - low_moving.shape[1]), F32)], axis=1)
    moving += [up[:, part * lanes : (part + 1) * lanes] for part in range(whole)]
    moving += [jnp.concatenate([left, up[:, whole * lanes :]], axis=1)]
    aux[...] = jnp.concatenate(moving, axis=0).astype(BF16)
    occ = column_of(plan, OCCUPIED, count, current.shape[1])
    last = jnp.zeros((count, current.shape[1]), F32)
    for slot in range(4):
        last = jnp.where(occ == slot + 1, live[slot * count : (slot + 1) * count], last)
    entries[pl.ds(0, count), :] = last
    time_last[...] = entries[pl.ds(0, count), pl.ds(pl.multiple_of(me * feature, feature), feature)]


def recur_kernel(
    plan, moved, hist_first, hist_low, rebuilt, a_r, a_k, a_v, a_l, w_right, base, reward, gain, w_out,
    next_state, partial, up_first,
):
    count = next_state.shape[0]
    channels = a_r.shape[1]
    place = [plan[PLACE + index] for index in range(count)]
    slots = column_of(plan, PLACE, count, channels)
    aux = moved[pl.ds(count * WIDTH, AUX * count), :].astype(F32)
    block = lambda part: aux[part * count : (part + 1) * count]
    inner = hist_low.shape[1]

    def with_first(rows, extra, hist):
        for slot in range(REB):
            extra = jnp.where(slots[:, : extra.shape[1]] == slot, hist[slot : slot + 1, :], extra)
        return jnp.concatenate([rows[:count] + extra, rows[count:]], axis=0)

    received = with_first(a_r[...], block(0), hist_first[0])
    keys = with_first(a_k[...], block(1), hist_first[1])
    values = with_first(a_v[...], block(2), hist_first[2])
    low = jnp.tanh(with_first(a_l[...], block(6)[:, :inner], hist_low[...])).astype(BF16)
    up_first[...] = jnp.concatenate([block(3), block(4), block(5), block(6)[:, channels // 2 :]], axis=1)
    decay = jnp.exp(-jnp.exp(base[...] + dot(low, w_right[...])))
    occ = column_of(plan, OCCUPIED, count, channels)
    slot_of = lambda rows: [rows[slot * count : (slot + 1) * count] for slot in range(4)]
    r, k, v, d = slot_of(received), slot_of(keys), slot_of(values), slot_of(decay)
    d = [jnp.where(occ > slot, d[slot], 1.0) for slot in range(4)]
    k_live = [jnp.where(occ > slot, k[slot], 0.0) for slot in range(4)]
    before = [jnp.ones_like(d[0])]
    for slot in range(4):
        before.append(before[-1] * d[slot])
    query = jnp.concatenate([r[slot] * before[slot] for slot in range(4)], axis=0)
    scores, pairs = [], []
    for slot in range(4):
        scores.append(r[slot] * reward[...] * k[slot])
        pairs.append((slot, slot))
        between = jnp.ones_like(d[0])
        for earlier in range(slot - 1, -1, -1):
            scores.append(r[slot] * between * k_live[earlier])
            pairs.append((slot, earlier))
            between = between * d[earlier]
    sums = head_sums(jnp.concatenate(scores, axis=0))
    inner = [jnp.zeros_like(v[0])] * 4
    for index, (slot, earlier) in enumerate(pairs):
        inner[slot] = inner[slot] + sums[index * count : (index + 1) * count] * v[earlier]
    mixed = jnp.concatenate(inner, axis=0)
    after = jnp.ones_like(d[0])
    k_after = [None] * 4
    for slot in range(3, -1, -1):
        k_after[slot] = k_live[slot] * after
        after = after * d[slot]
    k_high, k_low = halves(jnp.concatenate(k_after, axis=0))
    v_high, v_low = halves(values)
    k_rows = jnp.concatenate([k_high, k_high, k_low], axis=0)
    v_rows = jnp.concatenate([v_high, v_low, v_high], axis=0).astype(F32)
    k_columns = jnp.transpose(k_rows.astype(F32)).astype(BF16)
    after_columns = jnp.transpose(before[4])
    q_high, q_low = halves(query)
    q_rows = jnp.concatenate([q_high, q_low], axis=0).astype(F32)
    q_request = iota(q_rows.shape, 0) % count
    v_request = iota(v_rows.shape, 0) % count
    blocks = head_blocks(channels)
    total = jnp.zeros((q_rows.shape[0], channels), F32)
    for index in range(count):
        packed = moved[pl.ds(index * WIDTH, WIDTH), :].astype(F32)
        for slot in range(REB):
            packed = jnp.where(place[index] == slot, rebuilt[slot], packed)
        tall = jnp.concatenate([packed] * (channels // WIDTH), axis=0)
        tall = jnp.where(blocks, tall, 0.0).astype(BF16)
        total = total + dot(jnp.where(q_request == index, q_rows, 0.0).astype(BF16), tall)
        update = dot(k_columns, jnp.where(v_request == index, v_rows, 0.0).astype(BF16))
        for which in range(channels // WIDTH):
            rows = slice(which * WIDTH, (which + 1) * WIDTH)
            lanes = slice(which // 2 * 128, which // 2 * 128 + 128)
            block = update[rows, lanes] + after_columns[rows, index : index + 1] * packed[:, lanes]
            if which % 2:
                block = pltpu.roll(block, 64, 1)
            next_state[index, which] = block[:, :WIDTH]
    mixed = mixed + total[: 4 * count] + total[4 * count :]
    centered = mixed - head_sums(mixed) * (1.0 / WIDTH)
    spread = head_sums(centered * centered) * (1.0 / WIDTH)
    heads_out = (centered * lax.rsqrt(spread + EPSILON) * gain[...]).astype(BF16)
    partial[...] = dot(heads_out, w_out[...]).astype(BF16)


def ffn_kernel(
    plan, own, by_one, by_two, by_three, p_own, p_one, p_two, p_three, up_first, gain, rates,
    w_up, w_down,
    kept, to_one, to_two, to_three, channel_last,
    entries,
):
    ranks = 4
    feature = own.shape[1]
    tokens = p_own.shape[0]
    count = tokens // 4
    hist_rows = REB * 32
    me = lax.axis_index("head")
    for steps, piece in enumerate((own, by_one, by_two, by_three)):
        block = lax.rem(me - steps + ranks, ranks)
        entries[:, pl.ds(pl.multiple_of(block * feature, feature), feature)] = piece[
            pl.ds(hist_rows, tokens), :
        ].astype(F32)
    mix = sum(piece[...].astype(F32) for piece in (p_own, p_one, p_two, p_three))
    middle = (entries[...] + mix).astype(BF16).astype(F32)
    entries[...] = middle
    own_lanes = pl.ds(pl.multiple_of(me * feature, feature), feature)
    middle_own = entries[:, own_lanes]
    current = normalize(middle, gain[...])
    previous = jnp.concatenate([jnp.zeros_like(current[:count]), current[:-count]], axis=0)
    blended = (current + (previous - current) * rates[4:5, :]).astype(BF16)
    hidden = dot(blended, w_up[...])
    hidden = jnp.concatenate([hidden[:count] + up_first[...], hidden[count:]], axis=0)
    hidden = jnp.maximum(hidden, 0.0)
    hidden = (hidden * hidden).astype(BF16)
    for steps, target in enumerate((kept, to_one, to_two, to_three)):
        block = lax.rem(me + steps, ranks)
        lanes = pl.ds(pl.multiple_of(block * feature, feature), feature)
        rows = dot(hidden, w_down[:, lanes])
        if steps == 0:
            target[...] = rows + middle_own
        else:
            target[...] = rows.astype(BF16)
    occ = column_of(plan, OCCUPIED, count, current.shape[1])
    last = jnp.zeros((count, current.shape[1]), F32)
    for slot in range(4):
        last = jnp.where(occ == slot + 1, current[slot * count : (slot + 1) * count], last)
    entries[pl.ds(0, count), :] = last
    channel_last[...] = entries[pl.ds(0, count), own_lanes]


def on_device(
    arriving_hiddens,
    occupied_slot_totals,
    former_indices,
    reconstruct_marks,
    retained_hiddens,
    carried_memory_matrices,
    lagged_previous_entries,
    pre_attention_scaling,
    pre_feedforward_scaling,
    lag_blend_fractions,
    acceptance_projection,
    address_projection,
    content_projection,
    fading_lowrank_left,
    fading_lowrank_right,
    fading_baseline_entries,
    present_item_reward,
    grouped_layer_scaling,
    attention_exit_projection,
    feedforward_address_proj,
    feedforward_content_proj,
):
    count, steps, feature = arriving_hiddens.shape
    heads = carried_memory_matrices.shape[1]
    channels = heads * WIDTH
    hist = retained_hiddens.shape[1]
    model = pre_attention_scaling.shape[0]
    tokens = count * steps
    row = lambda value: value.reshape(1, -1)
    home, seated, aux_rows = count * WIDTH, SEATS * WIDTH, AUX * count
    far_weights = (
        acceptance_projection,
        address_projection,
        content_projection,
        fading_lowrank_left.T,
    )
    gathered, plus, minus, stay, *weights, plan = call(
        pack_kernel,
        "pack",
        (
            out((REB * hist + tokens + 2 * count, feature), BF16),
            out((seated, channels), BF16),
            out((seated, channels), BF16),
            out((home, channels), BF16),
            *(out(value.shape, BF16) for value in far_weights),
            out((PLAN,), jnp.int32),
        ),
        [
            (former_indices, "scalars"),
            (reconstruct_marks, "scalars"),
            (occupied_slot_totals, "scalars"),
            (retained_hiddens, "any"),
            (carried_memory_matrices, "any"),
            (lagged_previous_entries, "load"),
            (arriving_hiddens, "load"),
            *((value, "any") for value in far_weights),
        ],
        [
            pltpu.VMEM((tokens + 2 * count, feature), F32),
            pltpu.VMEM((count, heads, WIDTH, WIDTH), F32),
            pltpu.SemaphoreType.DMA((REB,)),
            pltpu.SemaphoreType.DMA((count,)),
            pltpu.SemaphoreType.DMA((len(far_weights),)),
        ],
        (VMEM_SPEC,) * (4 + len(far_weights)) + (SMEM_SPEC,),
    )

    def send(stage, up, down):
        return rotate(up, "grp", -STRIDES[stage]), rotate(down, "grp", STRIDES[stage])

    plus, minus = send(0, plus, minus)
    pieces = [gathered] + [rotate(gathered, "head", k) for k in (1, 2, 3)]
    base = row(fading_baseline_entries)
    inner = fading_lowrank_left.shape[1]
    a_r, a_k, a_v, a_l, rebuilt, aux, hist_first, hist_low, time_last = call(
        project_kernel,
        "project",
        (
            out((tokens, channels), F32),
            out((tokens, channels), F32),
            out((tokens, channels), F32),
            out((tokens, inner), F32),
            out((REB, WIDTH, channels), F32),
            out((AUX * count, channels), BF16),
            out((3, count, channels), F32),
            out((count, inner), F32),
            out((count, feature), F32),
        ),
        [(plan, "smem")]
        + [(value, "vmem") for value in pieces]
        + [(row(pre_attention_scaling), "load"), (lag_blend_fractions, "load")]
        + [(value, "vmem") for value in weights]
        + [(feedforward_address_proj, "any"), (fading_lowrank_right, "load"), (base, "load")],
        [
            pltpu.VMEM((REB * hist + tokens + 2 * count, model), F32),
            pltpu.VMEM(feedforward_address_proj.shape, BF16),
            pltpu.SemaphoreType.DMA((1,)),
        ],
        cost=pl.CostEstimate(flops=20_000_000_000, transcendentals=0, bytes_accessed=8_000_000),
    )
    arrived = (plus, minus, stay, *send(0, aux, aux), aux)
    shape = lambda rows: out((rows + aux_rows, channels), BF16)
    for stage in range(STAGES):
        last = stage + 1 == STAGES
        merged = call(
            functools.partial(merge_kernel, stage, count, stage == 0),
            "merge",
            shape(home) if last else (shape(seated), shape(seated), shape(home)),
            [(plan, "smem")] + [(value, "vmem") for value in arrived],
        )
        if not last:
            arrived = (*send(stage + 1, *merged[:2]), merged[2])

    def move_all(moved, aux, plan, former, state):
        packed = call(
            pack_all_kernel,
            "pack_all",
            out((home, channels), BF16),
            [(former, "scalars"), (state, "any")],
            [pltpu.VMEM((count, heads, WIDTH, WIDTH), F32), pltpu.SemaphoreType.DMA((count,))],
        )
        moved = jnp.concatenate([packed, aux], axis=0)
        for stage in range(STAGES):
            moved = call(
                functools.partial(merge_all_kernel, stage, count),
                "merge_all",
                shape(home),
                [(plan, "smem")] + [(value, "load") for value in (*send(stage, moved, moved), moved)],
            )
        return moved

    moved = lax.cond(
        plan[OVER] > 0,
        move_all,
        lambda moved, *_: moved,
        merged,
        aux,
        plan,
        former_indices,
        carried_memory_matrices,
    )
    next_state, partial, up_first = call(
        recur_kernel,
        "recur",
        (
            out((count, heads, WIDTH, WIDTH), F32),
            out((tokens, model), BF16),
            out((count, feedforward_address_proj.shape[1]), F32),
        ),
        [(plan, "smem")]
        + [(value, "vmem") for value in (moved, hist_first, hist_low, rebuilt, a_r, a_k, a_v, a_l)]
        + [(fading_lowrank_right, "load"), (base, "load")]
        + [(row(present_item_reward), "load"), (row(grouped_layer_scaling), "load")]
        + [(attention_exit_projection, "vmem")],
    )
    partials = [partial] + [rotate(partial, "head", k) for k in (1, 2, 3)]
    ffn_weights, _ = lax.optimization_barrier(
        ((feedforward_address_proj, feedforward_content_proj), partial)
    )
    ffn_weights = call(
        fetch_kernel,
        "fetch",
        tuple(out(value.shape, BF16) for value in ffn_weights),
        [(value, "any") for value in ffn_weights],
        [pltpu.SemaphoreType.DMA((len(ffn_weights),))],
    )
    kept, to_one, to_two, to_three, channel_last = call(
        ffn_kernel,
        "ffn",
        (
            out((tokens, feature), F32),
            out((tokens, feature), BF16),
            out((tokens, feature), BF16),
            out((tokens, feature), BF16),
            out((count, feature), F32),
        ),
        [(plan, "smem")]
        + [(value, "vmem") for value in (*pieces, *partials, up_first)]
        + [(row(pre_feedforward_scaling), "load"), (lag_blend_fractions, "load")]
        + [(value, "vmem") for value in ffn_weights],
        [pltpu.VMEM((tokens, model), F32)],
    )
    arrived = [rotate(value, "head", k + 1) for k, value in enumerate((to_one, to_two, to_three))]
    result = kept + sum(value.astype(F32) for value in arrived)
    result = jnp.swapaxes(result.astype(BF16).reshape(steps, count, feature), 0, 1)
    valid_rows = jnp.arange(steps)[None, :] < occupied_slot_totals[:, None]
    result = jnp.where(valid_rows[..., None], result, jnp.zeros_like(result))
    return (result, next_state, jnp.stack([time_last, channel_last], axis=1))


def solution(mesh):
    placed = (
        P("grp", None, "head"),
        P("grp"),
        P("grp"),
        P("grp"),
        P("grp", None, "head"),
        P("grp", "head", None, None),
        P("grp", None, "head"),
        P(),
        P(),
        P(),
        P(None, "head"),
        P(None, "head"),
        P(None, "head"),
        P(),
        P(None, "head"),
        P("head"),
        P("head"),
        P("head"),
        P("head", None),
        P(None, "head"),
        P("head", None),
    )
    return jax.shard_map(
        on_device,
        mesh=mesh,
        in_specs=placed,
        out_specs=(P("grp", None, "head"), P("grp", "head", None, None), P("grp", None, "head")),
        check_vma=False,
    )
```
